32 devices in a mesh: clip: 2 (over y), tile: 4 (over z), tm: 2 (over x), chan: 2 (over core).
Axes of the slice: x: 2, y: 2, z: 4, core: 2. Of those that a mesh axis runs over, the one named last changes fastest.
Arguments:
- latent: bfloat16 [8, 8, 256, 128], P(('clip', 'tm'), 'tile', 'chan'), parts along dimension 0
- norm1_gain: float32 [256], P('chan'), may hold values from 0.25 to 1.75
- norm1_bias: float32 [256], P('chan'), may hold values from -3 to 3
- conv1_weight: bfloat16 [3, 3, 3, 256, 256], P(None, None, None, None, 'chan'), may hold values from -0.078125 to 0.078125
- conv1_bias: float32 [256], P('chan'), may hold values from -3 to 3
- norm2_gain: float32 [256], P('chan'), may hold values from 0.25 to 1.75
- norm2_bias: float32 [256], P('chan'), may hold values from -3 to 3
- conv2_weight: bfloat16 [3, 3, 3, 256, 256], P(None, None, None, None, 'chan'), may hold values from -0.078125 to 0.078125
- conv2_bias: float32 [256], P('chan'), may hold values from -3 to 3
Outputs:
- upsampled: bfloat16 [8, 16, 64, 256], P(('clip', 'tm'), 'tile', 'chan'), parts along dimension 0
The draws below stay inside these ranges and needn't reach their ends.
There are 2 independent parts, one for each index of `clip`. The reference program is written for one: setup_inputs(seed, part) draws one part's arguments, and reference() takes and returns one part's arrays. A program takes and returns all parts, laid end to end along the dimension named above; an argument that names none is the same for every part. Nothing has to cross between parts.
All inputs are finite; a program needn't handle non-finite values.
Results may differ from the reference program's by a relative error of at most 0.0026.
Values may be sent and summed in bfloat16 or wider, within the bound.
A program may use at most 64 MiB of HBM per device.

```python
import jax
import jax.numpy as jnp
from jax import lax

C = 256
GROUPS = 32
WIDE = 128
FRAMES = 4
HEIGHT = 8


def draw_latent(key, part):
    keys = jax.random.split(key, 3)
    shape = (FRAMES, HEIGHT, C, WIDE)
    rows = jnp.arange(HEIGHT, dtype=jnp.float32) / float(max(HEIGHT - 1, 1))
    rough = jax.random.uniform(keys[1], (HEIGHT,), jnp.float32, 0.6, 1.4)
    offset = jax.random.uniform(keys[2], (FRAMES, 1, C, 1), jnp.float32, -0.6, 0.6)
    base = jax.random.normal(keys[0], shape, jnp.float32)
    row_scale = jnp.exp(jnp.log(3.0) * rows) * rough
    values = base * row_scale[None, :, None, None] + offset
    return values.astype(jnp.bfloat16)


def block_scale(stream_key, dims, pieces, least, top_value):
    loudness = 1.0
    for axis_at, shards_of in pieces:
        steps = jax.random.uniform(jax.random.fold_in(jax.random.fold_in(stream_key, 6), axis_at), (shards_of,), jnp.float32, least / len(pieces), top_value / len(pieces))
        loudness = loudness * jnp.repeat(jnp.exp(steps), dims[axis_at] // shards_of).reshape((-1,) + (1,) * (len(dims) - 1 - axis_at))
    return loudness


def scatter_about(rng, extent, spread, most, cuts=(), held_as=jnp.bfloat16):
    values = spread * jax.random.normal(rng, extent, jnp.float32)
    if cuts:
        values = values * block_scale(rng, extent, cuts, -0.22, 0.18)
    return jnp.clip(values, -most, most).astype(held_as)


def setup_inputs(seed: int = 0, part: int = 0) -> dict:
    seeds = jax.random.split(jax.random.key(seed), 10)
    part_keys = jax.random.split(jax.random.fold_in(seeds[9], part), 10)
    return {
        "latent": draw_latent(jax.random.fold_in(jax.random.fold_in(seeds[9], part), 71), part),
        "norm1_gain": jnp.clip(1.0 + 0.15 * jax.random.normal(seeds[1], (C,), jnp.float32), 0.25, 1.75),
        "norm1_bias": scatter_about(seeds[2], (C,), 0.5, 3.0, ((0, 2),), jnp.float32),
        "conv1_weight": scatter_about(seeds[3], (3, 3, 3, C, C), (27 * C) ** -0.5, 0.078125, ((4, 2),)),
        "conv1_bias": scatter_about(seeds[4], (C,), 0.5, 3.0, ((0, 2),), jnp.float32),
        "norm2_gain": jnp.clip(1.0 + 0.15 * jax.random.normal(seeds[5], (C,), jnp.float32), 0.25, 1.75),
        "norm2_bias": scatter_about(seeds[6], (C,), 0.5, 3.0, ((0, 2),), jnp.float32),
        "conv2_weight": scatter_about(seeds[7], (3, 3, 3, C, C), (27 * C) ** -0.5, 0.078125, ((4, 2),)),
        "conv2_bias": scatter_about(seeds[8], (C,), 0.5, 3.0, ((0, 2),), jnp.float32),
    }


def causal_norm(field, gain, bias):
    frames, height, channels, columns = field.shape
    size = channels // GROUPS
    parts = field.reshape(frames, height, GROUPS, size, columns)
    totals = jnp.cumsum(lax.optimization_barrier(jnp.sum(parts, axis=(1, 3, 4))), axis=0)
    squares = jnp.cumsum(lax.optimization_barrier(jnp.sum(parts * parts, axis=(1, 3, 4))), axis=0)
    count = (jnp.arange(frames, dtype=jnp.float32) + 1.0) * float(height * size * columns)
    mean = totals / count[:, None]
    var = squares / count[:, None] - mean * mean
    scale = 1.0 / jnp.sqrt(var + 1e-06)
    normed = (parts - mean[:, None, :, None, None]) * scale[:, None, :, None, None]
    normed = normed.reshape(frames, height, channels, columns)
    return normed * gain[None, None, :, None] + bias[None, None, :, None]

def causal_conv(field, weight, bias):
    padded = jnp.concatenate([field[0:1], field[0:1], field], axis=0)
    source = jnp.transpose(padded, (2, 0, 1, 3))[None]
    result = lax.conv_general_dilated(source, weight, (1, 1, 1), ((0, 0), (1, 1), (1, 1)), dimension_numbers=('NCDHW', 'DHWIO', 'NCDHW'), preferred_element_type=jnp.float32)
    result = jnp.transpose(result[0], (1, 2, 0, 3))
    return result + bias[None, None, :, None]

def reference(latent, norm1_gain, norm1_bias, conv1_weight, conv1_bias, norm2_gain, norm2_bias, conv2_weight, conv2_bias):
    source = latent.astype(jnp.float32)
    first = jax.nn.silu(causal_norm(source, norm1_gain, norm1_bias)).astype(jnp.bfloat16)
    hidden = causal_conv(first, conv1_weight, conv1_bias)
    second = jax.nn.silu(causal_norm(hidden, norm2_gain, norm2_bias)).astype(jnp.bfloat16)
    mixed = source + causal_conv(second, conv2_weight, conv2_bias)
    frames, height, channels, columns = mixed.shape
    shaped = mixed.reshape(frames, height, channels // 4, 2, 2, columns)
    shaped = jnp.transpose(shaped, (0, 1, 3, 2, 5, 4))
    return shaped.reshape(frames, 2 * height, channels // 4, 2 * columns).astype(jnp.bfloat16)
```

```python
import functools

import jax
import jax.numpy as jnp
from jax import lax
from jax.experimental import pallas as pl
from jax.experimental.pallas import tpu as pltpu
from jax.sharding import PartitionSpec as P

MESH = pl.DeviceIdType.MESH
C = 256
GROUPS = 32
SIZE = C // GROUPS
F32 = jnp.float32
BF16 = jnp.bfloat16


def iota(shape, dim):
    return lax.broadcasted_iota(jnp.int32, shape, dim)


def kernel(
    tiles,
    blocks,
    latent,
    n1g,
    n1b,
    w1,
    c1b,
    n2g,
    n2b,
    w2,
    c2b,
    out,
    raw,
    w1v,
    w2v,
    lat,
    act1,
    act2,
    hid,
    edge,
    halo,
    mix,
    select,
    params,
    own_stats,
    stats,
    gains,
    biases,
    part,
    landed,
    l_sem,
    p_sem,
    w_sem,
    w_send,
    w_recv,
    x_send,
    z_send,
    a_recv,
    r_send,
    r_recv,
    h_send,
    h_recv,
    s_send,
    s_recv,
):
    peers = tiles * blocks
    tm = lax.axis_index("tm")
    tile = lax.axis_index("tile")
    core = lax.axis_index("chan")
    other = 1 - core
    me = tm * tiles + tile
    rows, local, wide = latent.shape[1:]

    def where_is(index):
        return {"tm": index // tiles, "tile": index % tiles}

    def remote(src, dst, send, recv, **device):
        return pltpu.make_async_remote_copy(
            src_ref=src, dst_ref=dst, send_sem=send, recv_sem=recv, device_id=device, device_id_type=MESH
        )

    load = pltpu.make_async_copy(latent, raw, l_sem.at[0])
    load.start()
    barrier = pltpu.get_barrier_semaphore()

    def greet(step, carry):
        pl.semaphore_signal(barrier, inc=1, device_id=where_is(lax.rem(me + step, peers)), device_id_type=MESH)
        return carry

    lax.fori_loop(1, peers, greet, 0)
    pl.semaphore_signal(barrier, inc=1, device_id={"chan": other}, device_id_type=MESH)
    param_loads = [
        pltpu.make_async_copy(ref, params.at[i], p_sem.at[i]) for i, ref in enumerate((n1g, n1b, n2g, n2b, c1b, c2b))
    ]
    for copy in param_loads:
        copy.start()

    def own_half(w, wv, i):
        return pltpu.make_async_copy(
            w.at[:, pl.ds(pl.multiple_of(core * local, local), local)], wv.at[:, :, pl.ds(0, local)], w_sem.at[i]
        )

    def other_half(w, wv, i):
        return remote(
            w.at[:, pl.ds(pl.multiple_of(other * local, local), local)], wv.at[:, :, pl.ds(local, local)],
            w_send.at[i], w_recv.at[i], chan=other,
        )

    own_half(w1, w1v, 0).start()
    own_half(w2, w2v, 1).start()

    has_up = tile < tiles - 1
    has_down = tile > 0
    slots = [s for s in range(3) if blocks > 2 - s]
    before = [s for s in slots if s < 2]

    def stats_copy(which, to):
        return remote(own_stats.at[which], stats.at[which, me], s_send.at[which], s_recv.at[which], **where_is(to))

    def put_stats(which, rows_of):
        for i, row in enumerate(rows_of):
            own_stats[which, i:i + 1] = row
            stats[which, me, i:i + 1] = row

    def send_stats(which):
        def send(step, carry):
            stats_copy(which, lax.rem(me + step, peers)).start()
            return carry

        lax.fori_loop(1, peers, send, 0)

    def all_stats(which):
        whole = stats.at[which, pl.ds(0, peers - 1)]
        return remote(whole, whole, s_send.at[which], s_recv.at[which], chan=other)

    def group_sum(v):
        lane = iota(v.shape, 1)
        for step in (1, 2, 4):
            v = v + jnp.where(lane % (2 * step) < step, pltpu.roll(v, 128 - step, 1), pltpu.roll(v, step, 1))
        return v

    def make_norms(which, frames, gain, bias, shift):
        ahead = frames // 2 - 1
        e = iota((8, 128), 0)
        block = tm - ahead + e // 2
        later = jnp.logical_and(block >= 0, e % 2 == 1)
        block = jnp.maximum(block, 0)
        total = jnp.zeros((8, 128), F32)
        square = jnp.zeros((8, 128), F32)
        for b in range(blocks):
            s = jnp.sum(stats[which, pl.ds(b * tiles, tiles)], axis=0)
            first = b <= block
            second = jnp.logical_or(b < block, jnp.logical_and(b == block, later))
            total = total + jnp.where(first, s[0:1], 0.0) + jnp.where(second, s[1:2], 0.0)
            square = square + jnp.where(first, s[2:3], 0.0) + jnp.where(second, s[3:4], 0.0)
        number = (block * 2 + later.astype(jnp.int32) + 1).astype(F32)
        count = number * float(rows * tiles * SIZE * wide)
        mean = group_sum(total) / count
        var = group_sum(square) / count - mean * mean
        scale = 1.0 / jnp.sqrt(var + 1e-06)
        g = scale * (0.5 * gain)
        gains[which] = g
        biases[which] = 0.5 * bias + (shift - mean) * g

    at = iota((wide, local), 0)

    def norm_into(act, row, e, v, which):
        half = v * gains[which, pl.ds(e, 1)] + biases[which, pl.ds(e, 1)]
        v = half + half * jnp.tanh(half)
        act[0, row, e] = jnp.where(at == 0, 0.0, pltpu.roll(v, 1, 0)).astype(BF16)
        act[1, row, e] = v.astype(BF16)
        act[2, row, e] = jnp.where(at == wide - 1, 0.0, pltpu.roll(v, wide - 1, 0)).astype(BF16)

    def clear_edges(act):
        for side, row in ((has_down, 0), (has_up, 3)):
            @pl.when(jnp.logical_not(side))
            def _(row=row):
                act[:, row] = jnp.zeros((3,) + act.shape[2:], BF16)

    def conv(act, wv, o, first):
        lhs = jnp.concatenate(
            [
                jnp.concatenate(
                    [
                        act[k, r + j, jnp.maximum(o + i, first)]
                        for i in range(3) for j in range(3) for k in range(3)
                    ],
                    axis=1,
                )
                for r in range(2)
            ],
            axis=0,
        )
        return jnp.dot(lhs, wv[...].reshape(27 * local, C), preferred_element_type=F32)

    load.wait()
    sums = []
    for f in range(2):
        total = jnp.zeros((wide, local), F32)
        square = jnp.zeros((wide, local), F32)
        for r in range(2):
            t = raw[f, r].T
            lat[2, 1 + r, f] = t
            v = t.astype(F32)
            total = total + v
            square = square + v * v
        sums.append((jnp.sum(total, axis=0, keepdims=True), jnp.sum(square, axis=0, keepdims=True)))
    put_stats(0, (sums[0][0], sums[1][0], sums[0][1], sums[1][1]))
    pl.semaphore_wait(barrier, peers)
    send_stats(0)

    def lat_x(s, r, f):
        return remote(
            lat.at[2, 1 + r, f], lat.at[s, 1 + r, f], x_send.at[s], a_recv.at[s, 1 + r, f], tm=tm + (2 - s)
        )

    def lat_z(s, r, f):
        to, row = ((tile - 1, 3), (tile + 1, 0))[r]
        return remote(lat.at[s, 1 + r, f], lat.at[s, row, f], z_send.at[s, r], a_recv.at[s, row, f], tile=to)

    def side_of(r):
        return (has_down, has_up)[r]

    for s in reversed(before):
        @pl.when(tm + (2 - s) < blocks)
        def _(s=s):
            for f in range(2):
                for r in range(2):
                    lat_x(s, r, f).start()

    for r in range(2):
        @pl.when(side_of(r))
        def _(r=r):
            for f in range(2):
                lat_z(2, r, f).start()

    other_half(w1, w1v, 0).start()
    a, b = iota((2 * wide, 2 * wide), 0), iota((2 * wide, 2 * wide), 1)
    select[...] = jnp.where(b == 2 * (a % wide) + a // wide, 1.0, 0.0).astype(BF16)
    clear_edges(act1)
    clear_edges(act2)

    for s in reversed(before):
        @pl.when(tm >= 2 - s)
        def _(s=s):
            for f in range(2):
                for r in range(2):
                    lat_x(s, r, f).wait_recv()

                    @pl.when(side_of(r))
                    def _():
                        lat_z(s, r, f).start()

    other_half(w2, w2v, 1).start()
    for copy in param_loads:
        copy.wait()
    all_stats(0).wait_recv()
    make_norms(0, 6, params[0], params[1], 0.0)

    def wait_side(s, r):
        row = (0, 3)[r]
        for f in range(2):
            remote(lat.at[s, 1, f], lat.at[s, row, f], z_send.at[s, r], a_recv.at[s, row, f], chan=other).wait_recv()

    def norm1(s, rows_of):
        def one(f, carry):
            for row in rows_of:
                norm_into(act1, row, 2 * s + f, lat[s, row, f].astype(F32), 0)
            return carry

        lax.fori_loop(0, 2, one, 0)

    norm1(2, (1, 2))
    for r in range(2):
        @pl.when(side_of(r))
        def _(r=r):
            wait_side(2, r)
            norm1(2, ((0, 3)[r],))

    for s in reversed(before):
        @pl.when(tm >= 2 - s)
        def _(s=s):
            norm1(s, (1, 2))
            for r in range(2):
                @pl.when(side_of(r))
                def _(r=r):
                    wait_side(s, r)
                    norm1(s, ((0, 3)[r],))

    own_half(w1, w1v, 0).wait()
    other_half(w1, w1v, 0).wait_recv()
    first1 = 4 - 2 * jnp.minimum(tm, 2)
    first2 = 2 - 2 * jnp.minimum(tm, 1)

    def swap(o):
        return remote(part.at[o], landed.at[o], r_send.at[o], r_recv.at[o], chan=other)

    def conv1(o, carry):
        res = conv(act1, w1v, o, first1)
        hid[o] = res[:, :local]
        part[o] = res[:, local:]
        swap(o).start()
        return carry

    def edge_copy(o, r):
        to, side = ((tile - 1, 1), (tile + 1, 0))[r]
        return remote(edge.at[r, o], halo.at[side, o], h_send.at[r, o], h_recv.at[side, o], tile=to)

    def whole(o):
        swap(o).wait_recv()
        h = hid[o] + landed[o]
        hid[o] = h
        for r in range(2):
            edge[r, o] = h[r * wide:(r + 1) * wide].astype(BF16)

            @pl.when(side_of(r))
            def _(r=r):
                edge_copy(o, r).start()

        return h

    lax.fori_loop(2, 4, conv1, 0)
    sums = []
    for o in (2, 3):
        v = whole(o) + params[4]
        sums.append((jnp.sum(v, axis=0, keepdims=True), jnp.sum(v * v, axis=0, keepdims=True)))
    put_stats(1, (sums[0][0], sums[1][0], sums[0][1], sums[1][1]))
    send_stats(1)

    @pl.when(tm >= 1)
    def _():
        lax.fori_loop(0, 2, conv1, 0)
        for o in (0, 1):
            whole(o)

    def sent():
        all_stats(0).wait_send()
        for s in before:
            @pl.when(tm + (2 - s) < blocks)
            def _(s=s):
                own = lat.at[2, pl.ds(1, 2)]
                remote(own, own, x_send.at[s], a_recv.at[s, 1, 0], chan=other).wait_send()

        for s in slots:
            for r in range(2):
                @pl.when(jnp.logical_and(side_of(r), tm >= 2 - s))
                def _(s=s, r=r):
                    pair = lat.at[s, 1 + r]
                    remote(pair, pair, z_send.at[s, r], a_recv.at[s, 1, 0], chan=other).wait_send()

        for i, (w, wv) in enumerate(((w1, w1v), (w2, w2v))):
            other_half(w, wv, i).wait_send()

    sent()
    own_half(w2, w2v, 1).wait()
    other_half(w2, w2v, 1).wait_recv()
    all_stats(1).wait_recv()
    make_norms(1, 4, params[2], params[3], params[4])

    def norm2(e, carry):
        for r in range(2):
            norm_into(act2, 1 + r, e, hid[e, r * wide:(r + 1) * wide], 1)
        return carry

    def norm2_side(side, r, e):
        edge_from = remote(edge.at[r, e], halo.at[side, e], h_send.at[r, e], h_recv.at[side, e], chan=other)
        edge_from.wait_recv()
        norm_into(act2, (0, 3)[side], e, halo[side, e].astype(F32), 1)

    def norms2(first):
        lax.fori_loop(first, first + 2, norm2, 0)
        for side in range(2):
            @pl.when((has_down, has_up)[side])
            def _(side=side):
                def one(e, carry):
                    norm2_side(side, 1 - side, e)
                    return carry

                lax.fori_loop(first, first + 2, one, 0)

    norms2(2)
    pl.when(tm >= 1)(lambda: norms2(0))

    def conv2(o, carry):
        res = conv(act2, w2v, o, first2)
        hid[o] = res[:, :local]
        part[4 + o] = res[:, local:]
        swap(4 + o).start()
        return carry

    lax.fori_loop(0, 2, conv2, 0)

    spread = select[...]
    for f in range(2):
        swap(4 + f).wait_recv()
        for r in range(2):
            at_row = slice(r * wide, (r + 1) * wide)
            v = lat[2, 1 + r, f].astype(F32) + (hid[f, at_row] + landed[4 + f, at_row] + params[5])
            mix[f * 2 + r] = v.T
            for p in range(2):
                pair = [mix[f * 2 + r, pl.ds(2 * p + q, local // 4, stride=4), :].astype(BF16) for q in range(2)]
                out[f, 2 * r + p] = jnp.dot(
                    jnp.concatenate(pair, axis=1), spread, preferred_element_type=F32
                ).astype(BF16)

    all_stats(1).wait_send()
    for o in (2, 3, 4, 5):
        swap(o).wait_send()
    for r in range(2):
        @pl.when(side_of(r))
        def _(r=r):
            for o in (2, 3):
                edge_copy(o, r).wait_send()

    @pl.when(tm >= 1)
    def _():
        for o in (0, 1):
            swap(o).wait_send()
        for r in range(2):
            @pl.when(side_of(r))
            def _(r=r):
                for o in (0, 1):
                    edge_copy(o, r).wait_send()


def shards(tiles, blocks, latent, n1g, n1b, w1, c1b, n2g, n2b, w2, c2b):
    frames, rows, local, wide = latent.shape
    peers = tiles * blocks
    vmem = pl.BlockSpec(memory_space=pltpu.VMEM)
    hbm = pl.BlockSpec(memory_space=pl.ANY)
    dma = pltpu.SemaphoreType.DMA
    here = lambda v: pltpu.with_memory_space_constraint(v, pltpu.HBM)
    row = lambda v: here(v.reshape(1, local))
    taps = lambda v: here(v.reshape(27, C, local))
    return pl.pallas_call(
        functools.partial(kernel, tiles, blocks),
        out_shape=jax.ShapeDtypeStruct((frames, 2 * rows, local // 4, 2 * wide), BF16),
        in_specs=[hbm] * 9,
        out_specs=vmem,
        scratch_shapes=[
            pltpu.VMEM(latent.shape, BF16),
            pltpu.VMEM((27, local, C), BF16),
            pltpu.VMEM((27, local, C), BF16),
            pltpu.VMEM((3, 4, 2, wide, local), BF16),
            pltpu.VMEM((3, 4, 6, wide, local), BF16),
            pltpu.VMEM((3, 4, 4, wide, local), BF16),
            pltpu.VMEM((4, 2 * wide, local), F32),
            pltpu.VMEM((2, 4, wide, local), BF16),
            pltpu.VMEM((2, 4, wide, local), BF16),
            pltpu.VMEM((4, local, wide), F32),
            pltpu.VMEM((2 * wide, 2 * wide), BF16),
            pltpu.VMEM((6, 1, local), F32),
            pltpu.VMEM((2, 4, local), F32),
            pltpu.VMEM((2, peers, 4, local), F32),
            pltpu.VMEM((2, 8, local), F32),
            pltpu.VMEM((2, 8, local), F32),
            pltpu.VMEM((6, 2 * wide, local), F32),
            pltpu.VMEM((6, 2 * wide, local), F32),
            dma((1,)),
            dma((6,)),
            dma((2,)),
            dma((2,)),
            dma((2,)),
            dma((2,)),
            dma((3, 2)),
            dma((3, 4, 2)),
            dma((6,)),
            dma((6,)),
            dma((2, 4)),
            dma((2, 4)),
            dma((2,)),
            dma((2,)),
        ],
        compiler_params=pltpu.CompilerParams(
            collective_id=0, has_side_effects=True, vmem_limit_bytes=48 * 1024 * 1024
        ),
        name="block",
    )(here(latent), row(n1g), row(n1b), taps(w1), row(c1b), row(n2g), row(n2b), taps(w2), row(c2b))


def solution(mesh):
    return jax.shard_map(
        functools.partial(shards, mesh.shape["tile"], mesh.shape["tm"]),
        mesh=mesh,
        in_specs=(
            P(("clip", "tm"), "tile", "chan", None),
            P("chan"),
            P("chan"),
            P(None, None, None, None, "chan"),
            P("chan"),
            P("chan"),
            P("chan"),
            P(None, None, None, None, "chan"),
            P("chan"),
        ),
        out_specs=P(("clip", "tm"), "tile", "chan", None),
        check_vma=False,
    )
```

```python
import functools

import jax
import jax.numpy as jnp
from jax import lax
from jax.experimental import pallas as pl
from jax.experimental.pallas import tpu as pltpu
from jax.sharding import PartitionSpec as P

MESH = pl.DeviceIdType.MESH
C = 256
GROUPS = 32
SIZE = C // GROUPS
F32 = jnp.float32
BF16 = jnp.bfloat16


def iota(shape, dim):
    return lax.broadcasted_iota(jnp.int32, shape, dim)


def kernel(
    tiles,
    blocks,
    latent,
    n1g,
    n1b,
    w1,
    c1b,
    n2g,
    n2b,
    w2,
    c2b,
    out,
    raw,
    w1v,
    w2v,
    lat,
    act1,
    act2,
    acc,
    hid,
    edge,
    halo,
    mix,
    select,
    params,
    own_stats,
    stats,
    gains,
    biases,
    part,
    landed,
    l_sem,
    p_sem,
    w_sem,
    w_send,
    w_recv,
    x_send,
    z_send,
    a_recv,
    r_send,
    r_recv,
    h_send,
    h_recv,
    s_send,
    s_recv,
    x_turn,
):
    peers = tiles * blocks
    tm = lax.axis_index("tm")
    tile = lax.axis_index("tile")
    core = lax.axis_index("chan")
    other = 1 - core
    me = tm * tiles + tile
    rows, local, wide = latent.shape[1:]

    def where_is(index):
        return {"tm": index // tiles, "tile": index % tiles}

    def remote(src, dst, send, recv, **device):
        return pltpu.make_async_remote_copy(
            src_ref=src, dst_ref=dst, send_sem=send, recv_sem=recv, device_id=device, device_id_type=MESH
        )

    load = pltpu.make_async_copy(latent, raw, l_sem.at[0])
    load.start()
    barrier = pltpu.get_barrier_semaphore()

    def greet(step, carry):
        pl.semaphore_signal(barrier, inc=1, device_id=where_is(lax.rem(me + step, peers)), device_id_type=MESH)
        return carry

    lax.fori_loop(1, peers, greet, 0)
    pl.semaphore_signal(barrier, inc=1, device_id={"chan": other}, device_id_type=MESH)
    param_loads = [
        pltpu.make_async_copy(ref, params.at[i], p_sem.at[i]) for i, ref in enumerate((n1g, n1b, n2g, n2b, c1b, c2b))
    ]
    for copy in param_loads:
        copy.start()

    def own_half(w, wv, i):
        return pltpu.make_async_copy(
            w.at[:, pl.ds(pl.multiple_of(core * local, local), local)], wv.at[:, :, pl.ds(0, local)], w_sem.at[i]
        )

    def other_half(w, wv, i):
        return remote(
            w.at[:, pl.ds(pl.multiple_of(other * local, local), local)], wv.at[:, :, pl.ds(local, local)],
            w_send.at[i], w_recv.at[i], chan=other,
        )

    own_half(w1, w1v, 0).start()
    own_half(w2, w2v, 1).start()

    has_up = tile < tiles - 1
    has_down = tile > 0
    slots = [s for s in range(3) if blocks > 2 - s]
    before = [s for s in slots if s < 2]

    def stats_copy(which, to):
        return remote(own_stats.at[which], stats.at[which, me], s_send.at[which], s_recv.at[which], **where_is(to))

    def put_stats(which, rows_of):
        for i, row in enumerate(rows_of):
            own_stats[which, i:i + 1] = row
            stats[which, me, i:i + 1] = row

    def send_stats(which):
        def send(step, carry):
            stats_copy(which, lax.rem(me + step, peers)).start()
            return carry

        lax.fori_loop(1, peers, send, 0)

    def all_stats(which):
        whole = stats.at[which, pl.ds(0, peers - 1)]
        return remote(whole, whole, s_send.at[which], s_recv.at[which], chan=other)

    def group_sum(v):
        lane = iota(v.shape, 1)
        for step in (1, 2, 4):
            v = v + jnp.where(lane % (2 * step) < step, pltpu.roll(v, 128 - step, 1), pltpu.roll(v, step, 1))
        return v

    def make_norms(which, frames, gain, bias, shift):
        ahead = frames // 2 - 1
        e = iota((8, 128), 0)
        block = tm - ahead + e // 2
        later = jnp.logical_and(block >= 0, e % 2 == 1)
        block = jnp.maximum(block, 0)
        total = jnp.zeros((8, 128), F32)
        square = jnp.zeros((8, 128), F32)
        for b in range(blocks):
            s = jnp.sum(stats[which, pl.ds(b * tiles, tiles)], axis=0)
            first = b <= block
            second = jnp.logical_or(b < block, jnp.logical_and(b == block, later))
            total = total + jnp.where(first, s[0:1], 0.0) + jnp.where(second, s[1:2], 0.0)
            square = square + jnp.where(first, s[2:3], 0.0) + jnp.where(second, s[3:4], 0.0)
        number = (block * 2 + later.astype(jnp.int32) + 1).astype(F32)
        count = number * float(rows * tiles * SIZE * wide)
        mean = group_sum(total) / count
        var = group_sum(square) / count - mean * mean
        scale = 1.0 / jnp.sqrt(var + 1e-06)
        g = scale * (0.5 * gain)
        gains[which] = g
        biases[which] = 0.5 * bias + (shift - mean) * g

    at = iota((wide, local), 0)

    def norm_into(act, row, e, v, which):
        half = v * gains[which, pl.ds(e, 1)] + biases[which, pl.ds(e, 1)]
        v = half + half * jnp.tanh(half)
        act[0, row, e] = jnp.where(at == 0, 0.0, pltpu.roll(v, 1, 0)).astype(BF16)
        act[1, row, e] = v.astype(BF16)
        act[2, row, e] = jnp.where(at == wide - 1, 0.0, pltpu.roll(v, wide - 1, 0)).astype(BF16)

    def clear_edges(act):
        for side, row in ((has_down, 0), (has_up, 3)):
            @pl.when(jnp.logical_not(side))
            def _(row=row):
                act[:, row] = jnp.zeros((3,) + act.shape[2:], BF16)

    def taps(act, wv, o, first, rows_of, js):
        lhs = jnp.concatenate(
            [
                jnp.concatenate(
                    [act[k, row, jnp.maximum(o + f + i, first)] for row in rows_of for i in range(3) for k in range(3)],
                    axis=1,
                )
                for f in range(2)
            ],
            axis=0,
        )
        rhs = jnp.concatenate([wv[9 * i + 3 * j + k] for j in js for i in range(3) for k in range(3)], axis=0)
        return jnp.dot(lhs, rhs, preferred_element_type=F32)

    load.wait()
    sums = []
    for f in range(2):
        total = jnp.zeros((wide, local), F32)
        square = jnp.zeros((wide, local), F32)
        for r in range(2):
            t = raw[f, r].T
            lat[2, 1 + r, f] = t
            v = t.astype(F32)
            total = total + v
            square = square + v * v
        sums.append((jnp.sum(total, axis=0, keepdims=True), jnp.sum(square, axis=0, keepdims=True)))
    put_stats(0, (sums[0][0], sums[1][0], sums[0][1], sums[1][1]))
    pl.semaphore_wait(barrier, peers)
    send_stats(0)

    def lat_x(s, r, f):
        return remote(
            lat.at[2, 1 + r, f], lat.at[s, 1 + r, f], x_send.at[s], a_recv.at[s, 1 + r, f], tm=tm + (2 - s)
        )

    def lat_z(s, r, f):
        to, row = ((tile - 1, 3), (tile + 1, 0))[r]
        return remote(lat.at[s, 1 + r, f], lat.at[s, row, f], z_send.at[s, r], a_recv.at[s, row, f], tile=to)

    def side_of(r):
        return (has_down, has_up)[r]

    def send_x(s):
        for f in range(2):
            for r in range(2):
                lat_x(s, r, f).start()

    def sent_x(s):
        own = lat.at[2, pl.ds(1, 2)]
        remote(own, own, x_send.at[s], a_recv.at[s, 1, 0], chan=other).wait_send()

    def sends_x(s):
        return tm + (2 - s) < blocks

    for s in reversed(before):
        pl.when(jnp.logical_and(sends_x(s), core == 0))(lambda s=s: send_x(s))

    for r in range(2):
        @pl.when(side_of(r))
        def _(r=r):
            for f in range(2):
                lat_z(2, r, f).start()

    other_half(w1, w1v, 0).start()
    a, b = iota((2 * wide, 2 * wide), 0), iota((2 * wide, 2 * wide), 1)
    select[...] = jnp.where(b == 2 * (a % wide) + a // wide, 1.0, 0.0).astype(BF16)
    clear_edges(act1)
    clear_edges(act2)

    @pl.when(jnp.logical_and(sends_x(1), core == 0))
    def _():
        for s in before:
            pl.when(sends_x(s))(lambda s=s: sent_x(s))
        pl.semaphore_signal(x_turn, inc=1, device_id={"chan": other}, device_id_type=MESH)

    @pl.when(jnp.logical_and(sends_x(1), core == 1))
    def _():
        pl.semaphore_wait(x_turn, 1)
        for s in reversed(before):
            pl.when(sends_x(s))(lambda s=s: send_x(s))

    for s in reversed(before):
        @pl.when(tm >= 2 - s)
        def _(s=s):
            for f in range(2):
                for r in range(2):
                    lat_x(s, r, f).wait_recv()

                    @pl.when(side_of(r))
                    def _():
                        lat_z(s, r, f).start()

    other_half(w2, w2v, 1).start()
    for copy in param_loads:
        copy.wait()
    all_stats(0).wait_recv()
    make_norms(0, 6, params[0], params[1], 0.0)

    def wait_side(s, r):
        row = (0, 3)[r]
        for f in range(2):
            remote(lat.at[s, 1, f], lat.at[s, row, f], z_send.at[s, r], a_recv.at[s, row, f], chan=other).wait_recv()

    def norm1(s, rows_of):
        def one(f, carry):
            for row in rows_of:
                norm_into(act1, row, 2 * s + f, lat[s, row, f].astype(F32), 0)
            return carry

        lax.fori_loop(0, 2, one, 0)

    first1 = 4 - 2 * jnp.minimum(tm, 2)
    first2 = 2 - 2 * jnp.minimum(tm, 1)
    pairs = 1 + jnp.minimum(tm, 1)

    def norm1_sides(s):
        for r in range(2):
            @pl.when(side_of(r))
            def _(r=r):
                wait_side(s, r)
                norm1(s, ((0, 3)[r],))

    norm1(2, (1, 2))
    for s in reversed(before):
        pl.when(tm >= 2 - s)(lambda s=s: norm1(s, (1, 2)))
    own_half(w1, w1v, 0).wait()
    other_half(w1, w1v, 0).wait_recv()

    def inner(step, carry):
        p = 1 - step
        for r in range(2):
            acc[p, r] = taps(act1, w1v, 2 * p, first1, (1, 2), (1 - r, 2 - r))
        return carry

    lax.fori_loop(0, pairs, inner, 0)
    norm1_sides(2)
    for s in reversed(before):
        pl.when(tm >= 2 - s)(lambda s=s: norm1_sides(s))

    def swap(p, r):
        return remote(part.at[p, r], landed.at[p, r], r_send.at[p, r], r_recv.at[p, r], chan=other)

    def split(p, r, res):
        hid[p, r] = res[:, :local]
        part[p, r] = res[:, local:]
        swap(p, r).start()

    def outer(step, carry):
        p = 1 - step
        for r in range(2):
            split(p, r, acc[p, r] + taps(act1, w1v, 2 * p, first1, ((0, 3)[r],), (2 * r,)))
        return carry

    def edge_copy(p, r):
        to, side = ((tile - 1, 1), (tile + 1, 0))[r]
        return remote(edge.at[r, p], halo.at[side, p], h_send.at[r, p], h_recv.at[side, p], tile=to)

    def whole(p, r):
        swap(p, r).wait_recv()
        h = hid[p, r] + landed[p, r]
        hid[p, r] = h
        edge[r, p] = h.astype(BF16)
        pl.when(side_of(r))(lambda: edge_copy(p, r).start())
        return h + params[4]

    lax.fori_loop(0, pairs, outer, 0)
    both = [whole(1, r) for r in range(2)]
    total = both[0] + both[1]
    square = both[0] * both[0] + both[1] * both[1]
    frames_of = [slice(f * wide, (f + 1) * wide) for f in range(2)]
    put_stats(1, [jnp.sum(v[at_frame], axis=0, keepdims=True) for v in (total, square) for at_frame in frames_of])
    send_stats(1)

    @pl.when(tm >= 1)
    def _():
        for r in range(2):
            whole(0, r)

    def sent():
        all_stats(0).wait_send()
        @pl.when(core == 1)
        def _():
            for s in before:
                pl.when(sends_x(s))(lambda s=s: sent_x(s))

        for s in slots:
            for r in range(2):
                @pl.when(jnp.logical_and(side_of(r), tm >= 2 - s))
                def _(s=s, r=r):
                    pair = lat.at[s, 1 + r]
                    remote(pair, pair, z_send.at[s, r], a_recv.at[s, 1, 0], chan=other).wait_send()

        for i, (w, wv) in enumerate(((w1, w1v), (w2, w2v))):
            other_half(w, wv, i).wait_send()

    sent()
    own_half(w2, w2v, 1).wait()
    other_half(w2, w2v, 1).wait_recv()
    all_stats(1).wait_recv()
    make_norms(1, 4, params[2], params[3], params[4])

    def norm2(p, carry):
        for f in range(2):
            for r in range(2):
                norm_into(act2, 1 + r, 2 * p + f, hid[p, r, f * wide:(f + 1) * wide], 1)
        return carry

    def norms2(p):
        for side in range(2):
            @pl.when((has_down, has_up)[side])
            def _(side=side):
                source = edge.at[1 - side, p]
                remote(source, halo.at[side, p], h_send.at[1 - side, p], h_recv.at[side, p], chan=other).wait_recv()
                for f in range(2):
                    v = halo[side, p, f * wide:(f + 1) * wide].astype(F32)
                    norm_into(act2, (0, 3)[side], 2 * p + f, v, 1)

    def norms2_of(step, carry):
        norms2(1 - step)
        return carry

    lax.fori_loop(2 - pairs, 2, norm2, 0)
    lax.fori_loop(0, pairs, norms2_of, 0)

    def conv2(r, carry):
        split(2, r, taps(act2, w2v, 0, first2, (r, r + 1, r + 2), (0, 1, 2)))
        return carry

    lax.fori_loop(0, 2, conv2, 0)

    spread = select[...]
    for r in range(2):
        swap(2, r).wait_recv()
        for f in range(2):
            at_frame = slice(f * wide, (f + 1) * wide)
            v = lat[2, 1 + r, f].astype(F32) + (hid[2, r, at_frame] + landed[2, r, at_frame] + params[5])
            mix[f * 2 + r] = v.T
            for p in range(2):
                pair = [mix[f * 2 + r, pl.ds(2 * p + q, local // 4, stride=4), :].astype(BF16) for q in range(2)]
                out[f, 2 * r + p] = jnp.dot(
                    jnp.concatenate(pair, axis=1), spread, preferred_element_type=F32
                ).astype(BF16)

    all_stats(1).wait_send()
    for r in range(2):
        swap(1, r).wait_send()
        swap(2, r).wait_send()
        pl.when(side_of(r))(lambda r=r: edge_copy(1, r).wait_send())

    @pl.when(tm >= 1)
    def _():
        for r in range(2):
            swap(0, r).wait_send()
            pl.when(side_of(r))(lambda r=r: edge_copy(0, r).wait_send())


def shards(tiles, blocks, latent, n1g, n1b, w1, c1b, n2g, n2b, w2, c2b):
    frames, rows, local, wide = latent.shape
    peers = tiles * blocks
    vmem = pl.BlockSpec(memory_space=pltpu.VMEM)
    hbm = pl.BlockSpec(memory_space=pl.ANY)
    dma = pltpu.SemaphoreType.DMA
    here = lambda v: pltpu.with_memory_space_constraint(v, pltpu.HBM)
    row = lambda v: here(v.reshape(1, local))
    flat = lambda v: here(v.reshape(27, C, local))
    return pl.pallas_call(
        functools.partial(kernel, tiles, blocks),
        out_shape=jax.ShapeDtypeStruct((frames, 2 * rows, local // 4, 2 * wide), BF16),
        in_specs=[hbm] * 9,
        out_specs=vmem,
        scratch_shapes=[
            pltpu.VMEM(latent.shape, BF16),
            pltpu.VMEM((27, local, C), BF16),
            pltpu.VMEM((27, local, C), BF16),
            pltpu.VMEM((3, 4, 2, wide, local), BF16),
            pltpu.VMEM((3, 4, 6, wide, local), BF16),
            pltpu.VMEM((3, 4, 4, wide, local), BF16),
            pltpu.VMEM((2, 2, 2 * wide, C), F32),
            pltpu.VMEM((3, 2, 2 * wide, local), F32),
            pltpu.VMEM((2, 2, 2 * wide, local), BF16),
            pltpu.VMEM((2, 2, 2 * wide, local), BF16),
            pltpu.VMEM((4, local, wide), F32),
            pltpu.VMEM((2 * wide, 2 * wide), BF16),
            pltpu.VMEM((6, 1, local), F32),
            pltpu.VMEM((2, 4, local), F32),
            pltpu.VMEM((2, peers, 4, local), F32),
            pltpu.VMEM((2, 8, local), F32),
            pltpu.VMEM((2, 8, local), F32),
            pltpu.VMEM((3, 2, 2 * wide, local), F32),
            pltpu.VMEM((3, 2, 2 * wide, local), F32),
            dma((1,)),
            dma((6,)),
            dma((2,)),
            dma((2,)),
            dma((2,)),
            dma((2,)),
            dma((3, 2)),
            dma((3, 4, 2)),
            dma((3, 2)),
            dma((3, 2)),
            dma((2, 2)),
            dma((2, 2)),
            dma((2,)),
            dma((2,)),
            pltpu.SemaphoreType.REGULAR,
        ],
        compiler_params=pltpu.CompilerParams(
            collective_id=0, has_side_effects=True, vmem_limit_bytes=48 * 1024 * 1024
        ),
        name="block",
    )(here(latent), row(n1g), row(n1b), flat(w1), row(c1b), row(n2g), row(n2b), flat(w2), row(c2b))


def solution(mesh):
    return jax.shard_map(
        functools.partial(shards, mesh.shape["tile"], mesh.shape["tm"]),
        mesh=mesh,
        in_specs=(
            P(("clip", "tm"), "tile", "chan", None),
            P("chan"),
            P("chan"),
            P(None, None, None, None, "chan"),
            P("chan"),
            P("chan"),
            P("chan"),
            P(None, None, None, None, "chan"),
            P("chan"),
        ),
        out_specs=P(("clip", "tm"), "tile", "chan", None),
        check_vma=False,
    )
```

```python
import functools

import jax
import jax.numpy as jnp
from jax import lax
from jax.experimental import pallas as pl
from jax.experimental.pallas import tpu as pltpu
from jax.sharding import PartitionSpec as P

MESH = pl.DeviceIdType.MESH
C = 256
GROUPS = 32
SIZE = C // GROUPS
F32 = jnp.float32
BF16 = jnp.bfloat16


def iota(shape, dim):
    return lax.broadcasted_iota(jnp.int32, shape, dim)


def kernel(
    tiles,
    blocks,
    latent,
    n1g,
    n1b,
    w1,
    c1b,
    n2g,
    n2b,
    w2,
    c2b,
    out,
    raw,
    w1v,
    w2v,
    lat,
    act1,
    act2,
    acc,
    hid,
    edge,
    halo,
    mix,
    select,
    params,
    own_stats,
    stats,
    gains,
    biases,
    part,
    landed,
    l_sem,
    p_sem,
    w_sem,
    w_send,
    w_recv,
    x_send,
    z_send,
    a_recv,
    r_send,
    r_recv,
    h_send,
    h_recv,
    s_send,
    s_recv,
):
    tm = lax.axis_index("tm")
    tile = lax.axis_index("tile")
    core = lax.axis_index("chan")
    other = 1 - core
    me = tm * tiles + tile
    rows, local, wide = latent.shape[1:]

    def where_is(index):
        return {"tm": index // tiles, "tile": index % tiles}

    def remote(src, dst, send, recv, **device):
        return pltpu.make_async_remote_copy(
            src_ref=src, dst_ref=dst, send_sem=send, recv_sem=recv, device_id=device, device_id_type=MESH
        )

    load = pltpu.make_async_copy(latent, raw, l_sem.at[0])
    load.start()
    barrier = pltpu.get_barrier_semaphore()

    earlier = (tm + 1) * tiles
    later = (blocks - tm) * tiles

    def greet(step, carry):
        pl.semaphore_signal(barrier, inc=1, device_id=where_is(lax.rem(me + step, earlier)), device_id_type=MESH)
        return carry

    lax.fori_loop(1, earlier, greet, 0)
    pl.semaphore_signal(barrier, inc=1, device_id={"chan": other}, device_id_type=MESH)
    param_loads = [
        pltpu.make_async_copy(ref, params.at[i], p_sem.at[i]) for i, ref in enumerate((n1g, n1b, n2g, n2b, c1b, c2b))
    ]
    for copy in param_loads:
        copy.start()

    def own_half(w, wv, i):
        return pltpu.make_async_copy(
            w.at[:, pl.ds(pl.multiple_of(core * local, local), local)], wv.at[:, :, pl.ds(0, local)], w_sem.at[i]
        )

    def other_half(w, wv, i):
        return remote(
            w.at[:, pl.ds(pl.multiple_of(other * local, local), local)], wv.at[:, :, pl.ds(local, local)],
            w_send.at[i], w_recv.at[i], chan=other,
        )

    own_half(w1, w1v, 0).start()
    own_half(w2, w2v, 1).start()

    has_up = tile < tiles - 1
    has_down = tile > 0
    slots = [s for s in range(3) if blocks > 2 - s]
    before = [s for s in slots if s < 2]

    def put_stats(which, rows_of):
        for i, row in enumerate(rows_of):
            own_stats[which, i:i + 1] = row
            stats[which, me, i:i + 1] = row

    def send_stats(which):
        def send(step, carry):
            to = tm * tiles + lax.rem(tile + step, later)
            remote(own_stats.at[which], stats.at[which, me], s_send.at[which], s_recv.at[which, tm],
                   **where_is(to)).start()
            return carry

        lax.fori_loop(1, later, send, 0)

    def of_stats(which, b, n):
        some = stats.at[which, pl.ds(0, n)]
        return remote(some, some, s_send.at[which], s_recv.at[which, b], chan=other)

    def wait_stats(which):
        of_stats(which, tm, tiles - 1).wait_recv()
        for b in range(blocks - 1):
            pl.when(b < tm)(lambda b=b: of_stats(which, b, tiles).wait_recv())

    def sent_stats(which):
        of_stats(which, tm, tiles - 1).wait_send()
        for b in range(1, blocks):
            pl.when(b > tm)(lambda b=b: of_stats(which, b, tiles).wait_send())

    def group_sum(v):
        lane = iota(v.shape, 1)
        for step in (1, 2, 4):
            v = v + jnp.where(lane % (2 * step) < step, pltpu.roll(v, 128 - step, 1), pltpu.roll(v, step, 1))
        return v

    def make_norms(which, frames, gain, bias, shift):
        ahead = frames // 2 - 1
        e = iota((8, 128), 0)
        block = tm - ahead + e // 2
        odd = jnp.logical_and(block >= 0, e % 2 == 1)
        block = jnp.maximum(block, 0)
        total = jnp.zeros((8, 128), F32)
        square = jnp.zeros((8, 128), F32)
        for b in range(blocks):
            s = jnp.sum(stats[which, pl.ds(b * tiles, tiles)], axis=0)
            first = b <= block
            second = jnp.logical_or(b < block, jnp.logical_and(b == block, odd))
            total = total + jnp.where(first, s[0:1], 0.0) + jnp.where(second, s[1:2], 0.0)
            square = square + jnp.where(first, s[2:3], 0.0) + jnp.where(second, s[3:4], 0.0)
        number = (block * 2 + odd.astype(jnp.int32) + 1).astype(F32)
        count = number * float(rows * tiles * SIZE * wide)
        mean = group_sum(total) / count
        var = group_sum(square) / count - mean * mean
        scale = 1.0 / jnp.sqrt(var + 1e-06)
        g = scale * (0.5 * gain)
        gains[which] = g
        biases[which] = 0.5 * bias + (shift - mean) * g

    at = iota((wide, local), 0)

    def norm_into(act, row, e, v, which):
        half = v * gains[which, pl.ds(e, 1)] + biases[which, pl.ds(e, 1)]
        v = half + half * jnp.tanh(half)
        act[0, row, e] = jnp.where(at == 0, 0.0, pltpu.roll(v, 1, 0)).astype(BF16)
        act[1, row, e] = v.astype(BF16)
        act[2, row, e] = jnp.where(at == wide - 1, 0.0, pltpu.roll(v, wide - 1, 0)).astype(BF16)

    def clear_edges(act):
        for side, row in ((has_down, 0), (has_up, 3)):
            @pl.when(jnp.logical_not(side))
            def _(row=row):
                act[:, row] = jnp.zeros((3,) + act.shape[2:], BF16)

    def taps(act, wv, o, first, rows_of, js):
        lhs = jnp.concatenate(
            [
                jnp.concatenate(
                    [act[k, row, jnp.maximum(o + f + i, first)] for row in rows_of for i in range(3) for k in range(3)],
                    axis=1,
                )
                for f in range(2)
            ],
            axis=0,
        )
        rhs = jnp.concatenate([wv[9 * i + 3 * j + k] for j in js for i in range(3) for k in range(3)], axis=0)
        return jnp.dot(lhs, rhs, preferred_element_type=F32)

    load.wait()
    sums = []
    for f in range(2):
        total = jnp.zeros((wide, local), F32)
        square = jnp.zeros((wide, local), F32)
        for r in range(2):
            t = raw[f, r].T
            lat[2, 1 + r, f] = t
            v = t.astype(F32)
            total = total + v
            square = square + v * v
        sums.append((jnp.sum(total, axis=0, keepdims=True), jnp.sum(square, axis=0, keepdims=True)))
    put_stats(0, (sums[0][0], sums[1][0], sums[0][1], sums[1][1]))
    pl.semaphore_wait(barrier, later)

    def lat_x(s, r, f):
        return remote(
            lat.at[2, 1 + r, f], lat.at[s, 1 + r, f], x_send.at[s], a_recv.at[s, 1 + r, f], tm=tm + (2 - s)
        )

    def lat_z(s, r, f):
        to, row = ((tile - 1, 3), (tile + 1, 0))[r]
        return remote(lat.at[s, 1 + r, f], lat.at[s, row, f], z_send.at[s, r], a_recv.at[s, row, f], tile=to)

    def lat_xz(s, r, f):
        to, row = ((tile - 1, 3), (tile + 1, 0))[r]
        return remote(
            lat.at[2, 1 + r, f], lat.at[s, row, f], z_send.at[s, r], a_recv.at[s, row, f], tm=tm + (2 - s), tile=to
        )

    def side_of(r):
        return (has_down, has_up)[r]

    def send_x(s):
        for f in range(2):
            for r in range(2):
                lat_x(s, r, f).start()

    def send_xz(s):
        for f in range(2):
            for r in range(2):
                pl.when(side_of(r))(lambda f=f, r=r: lat_xz(s, r, f).start())

    def sent_x(s):
        own = lat.at[2, pl.ds(1, 2)]
        remote(own, own, x_send.at[s], a_recv.at[s, 1, 0], chan=other).wait_send()

    def sends_x(s):
        return tm + (2 - s) < blocks

    for s in reversed(before):
        pl.when(jnp.logical_and(sends_x(s), core == 0))(lambda s=s: send_x(s))

    send_stats(0)
    for r in range(2):
        @pl.when(side_of(r))
        def _(r=r):
            for f in range(2):
                lat_z(2, r, f).start()

    for s in reversed(before):
        pl.when(jnp.logical_and(sends_x(s), core == 0))(lambda s=s: send_xz(s))

    other_half(w1, w1v, 0).start()
    a, b = iota((2 * wide, 2 * wide), 0), iota((2 * wide, 2 * wide), 1)
    select[...] = jnp.where(b == 2 * (a % wide) + a // wide, 1.0, 0.0).astype(BF16)
    clear_edges(act1)
    clear_edges(act2)

    for s in reversed(before):
        pl.when(jnp.logical_and(sends_x(s), core == 1))(lambda s=s: send_x(s))

    for s in reversed(before):
        @pl.when(tm >= 2 - s)
        def _(s=s):
            for f in range(2):
                for r in range(2):
                    lat_x(s, r, f).wait_recv()

                    @pl.when(jnp.logical_and(side_of(r), core == 1))
                    def _():
                        lat_z(s, r, f).start()

    other_half(w2, w2v, 1).start()
    for copy in param_loads:
        copy.wait()
    wait_stats(0)
    make_norms(0, 6, params[0], params[1], 0.0)

    def wait_side(s, r):
        row = (0, 3)[r]
        for f in range(2):
            remote(lat.at[s, 1, f], lat.at[s, row, f], z_send.at[s, r], a_recv.at[s, row, f], chan=other).wait_recv()

    def norm1(s, rows_of):
        def one(f, carry):
            for row in rows_of:
                norm_into(act1, row, 2 * s + f, lat[s, row, f].astype(F32), 0)
            return carry

        lax.fori_loop(0, 2, one, 0)

    first1 = 4 - 2 * jnp.minimum(tm, 2)
    first2 = 2 - 2 * jnp.minimum(tm, 1)
    pairs = 1 + jnp.minimum(tm, 1)

    def norm1_sides(s):
        for r in range(2):
            @pl.when(side_of(r))
            def _(r=r):
                wait_side(s, r)
                norm1(s, ((0, 3)[r],))

    norm1(2, (1, 2))
    for s in reversed(before):
        pl.when(tm >= 2 - s)(lambda s=s: norm1(s, (1, 2)))
    own_half(w1, w1v, 0).wait()
    other_half(w1, w1v, 0).wait_recv()

    def inner(step, carry):
        p = 1 - step
        for r in range(2):
            acc[p, r] = taps(act1, w1v, 2 * p, first1, (1, 2), (1 - r, 2 - r))
        return carry

    lax.fori_loop(0, pairs, inner, 0)
    norm1_sides(2)
    for s in reversed(before):
        pl.when(tm >= 2 - s)(lambda s=s: norm1_sides(s))

    def swap(p, r):
        return remote(part.at[p, r], landed.at[p, r], r_send.at[p, r], r_recv.at[p, r], chan=other)

    def outer(step, carry):
        p = 1 - step
        for r in range(2):
            res = acc[p, r] + taps(act1, w1v, 2 * p, first1, ((0, 3)[r],), (2 * r,))
            hid[p, r] = res[:, :local]
            part[p, r] = res[:, local:]
        for r in range(2):
            swap(p, r).start()
        return carry

    def edge_copy(r):
        to, side = ((tile - 1, 1), (tile + 1, 0))[r]
        return remote(edge.at[r], halo.at[side, 1], h_send.at[r, 1], h_recv.at[side, 1], tile=to)

    def edge_next(r):
        to, side = ((tile - 1, 1), (tile + 1, 0))[r]
        return remote(edge.at[r], halo.at[side, 0], h_send.at[r, 0], h_recv.at[side, 0], tm=tm + 1, tile=to)

    def whole(p, r):
        swap(p, r).wait_recv()
        h = hid[p, r] + landed[p, r]
        hid[p, r] = h
        return h + params[4]

    lax.fori_loop(0, pairs, outer, 0)
    both = [whole(1, r) for r in range(2)]
    total = both[0] + both[1]
    square = both[0] * both[0] + both[1] * both[1]
    frames_of = [slice(f * wide, (f + 1) * wide) for f in range(2)]
    put_stats(1, [jnp.sum(v[at_frame], axis=0, keepdims=True) for v in (total, square) for at_frame in frames_of])
    send_stats(1)
    for r in range(2):
        edge[r] = hid[1, r].astype(BF16)
        pl.when(side_of(r))(lambda r=r: edge_copy(r).start())

    for r in range(2):
        pl.when(jnp.logical_and(side_of(r), sends_x(1)))(lambda r=r: edge_next(r).start())

    @pl.when(tm >= 1)
    def _():
        for r in range(2):
            whole(0, r)

    def sent():
        sent_stats(0)
        for s in before:
            pl.when(sends_x(s))(lambda s=s: sent_x(s))

        for s in slots:
            for r in range(2):
                @pl.when(jnp.logical_and(side_of(r), jnp.where(core == 1, tm >= 2 - s, sends_x(s))))
                def _(s=s, r=r):
                    pair = lat.at[s, 1 + r]
                    remote(pair, pair, z_send.at[s, r], a_recv.at[s, 1, 0], chan=other).wait_send()

        for i, (w, wv) in enumerate(((w1, w1v), (w2, w2v))):
            other_half(w, wv, i).wait_send()

    sent()
    own_half(w2, w2v, 1).wait()
    other_half(w2, w2v, 1).wait_recv()
    wait_stats(1)
    make_norms(1, 4, params[2], params[3], params[4])

    def norm2(p, carry):
        for f in range(2):
            for r in range(2):
                norm_into(act2, 1 + r, 2 * p + f, hid[p, r, f * wide:(f + 1) * wide], 1)
        return carry

    def norms2(p):
        for side in range(2):
            @pl.when((has_down, has_up)[side])
            def _(side=side):
                source = edge.at[1 - side]
                remote(source, halo.at[side, p], h_send.at[1 - side, p], h_recv.at[side, p], chan=other).wait_recv()
                for f in range(2):
                    v = halo[side, p, f * wide:(f + 1) * wide].astype(F32)
                    norm_into(act2, (0, 3)[side], 2 * p + f, v, 1)

    def norms2_of(step, carry):
        norms2(1 - step)
        return carry

    lax.fori_loop(2 - pairs, 2, norm2, 0)
    lax.fori_loop(0, pairs, norms2_of, 0)

    def conv2(r, carry):
        res = taps(act2, w2v, 0, first2, (r, r + 1, r + 2), (0, 1, 2))
        hid[2, r] = res[:, :local]
        part[2, r] = res[:, local:]
        swap(2, r).start()
        return carry

    lax.fori_loop(0, 2, conv2, 0)

    spread = select[...]
    for r in range(2):
        swap(2, r).wait_recv()
        for f in range(2):
            at_frame = slice(f * wide, (f + 1) * wide)
            v = lat[2, 1 + r, f].astype(F32) + (hid[2, r, at_frame] + landed[2, r, at_frame] + params[5])
            mix[f * 2 + r] = v.T
            for p in range(2):
                pair = [mix[f * 2 + r, pl.ds(2 * p + q, local // 4, stride=4), :].astype(BF16) for q in range(2)]
                out[f, 2 * r + p] = jnp.dot(
                    jnp.concatenate(pair, axis=1), spread, preferred_element_type=F32
                ).astype(BF16)

    sent_stats(1)
    for r in range(2):
        swap(1, r).wait_send()
        swap(2, r).wait_send()
        pl.when(tm >= 1)(lambda r=r: swap(0, r).wait_send())
        pl.when(side_of(r))(lambda r=r: edge_copy(r).wait_send())
        pl.when(jnp.logical_and(side_of(r), sends_x(1)))(lambda r=r: edge_next(r).wait_send())


def shards(tiles, blocks, latent, n1g, n1b, w1, c1b, n2g, n2b, w2, c2b):
    frames, rows, local, wide = latent.shape
    peers = tiles * blocks
    vmem = pl.BlockSpec(memory_space=pltpu.VMEM)
    hbm = pl.BlockSpec(memory_space=pl.ANY)
    dma = pltpu.SemaphoreType.DMA
    here = lambda v: pltpu.with_memory_space_constraint(v, pltpu.HBM)
    row = lambda v: here(v.reshape(1, local))
    flat = lambda v: here(v.reshape(27, C, local))
    return pl.pallas_call(
        functools.partial(kernel, tiles, blocks),
        out_shape=jax.ShapeDtypeStruct((frames, 2 * rows, local // 4, 2 * wide), BF16),
        in_specs=[hbm] * 9,
        out_specs=vmem,
        scratch_shapes=[
            pltpu.VMEM(latent.shape, BF16),
            pltpu.VMEM((27, local, C), BF16),
            pltpu.VMEM((27, local, C), BF16),
            pltpu.VMEM((3, 4, 2, wide, local), BF16),
            pltpu.VMEM((3, 4, 6, wide, local), BF16),
            pltpu.VMEM((3, 4, 4, wide, local), BF16),
            pltpu.VMEM((2, 2, 2 * wide, C), F32),
            pltpu.VMEM((3, 2, 2 * wide, local), F32),
            pltpu.VMEM((2, 2 * wide, local), BF16),
            pltpu.VMEM((2, 2, 2 * wide, local), BF16),
            pltpu.VMEM((4, local, wide), F32),
            pltpu.VMEM((2 * wide, 2 * wide), BF16),
            pltpu.VMEM((6, 1, local), F32),
            pltpu.VMEM((2, 4, local), F32),
            pltpu.VMEM((2, peers, 4, local), F32),
            pltpu.VMEM((2, 8, local), F32),
            pltpu.VMEM((2, 8, local), F32),
            pltpu.VMEM((3, 2, 2 * wide, local), F32),
            pltpu.VMEM((3, 2, 2 * wide, local), F32),
            dma((1,)),
            dma((6,)),
            dma((2,)),
            dma((2,)),
            dma((2,)),
            dma((2,)),
            dma((3, 2)),
            dma((3, 4, 2)),
            dma((3, 2)),
            dma((3, 2)),
            dma((2, 2)),
            dma((2, 2)),
            dma((2,)),
            dma((2, blocks)),
        ],
        compiler_params=pltpu.CompilerParams(
            collective_id=0, has_side_effects=True, vmem_limit_bytes=48 * 1024 * 1024
        ),
        name="block",
    )(here(latent), row(n1g), row(n1b), flat(w1), row(c1b), row(n2g), row(n2b), flat(w2), row(c2b))


def solution(mesh):
    return jax.shard_map(
        functools.partial(shards, mesh.shape["tile"], mesh.shape["tm"]),
        mesh=mesh,
        in_specs=(
            P(("clip", "tm"), "tile", "chan", None),
            P("chan"),
            P("chan"),
            P(None, None, None, None, "chan"),
            P("chan"),
            P("chan"),
            P("chan"),
            P(None, None, None, None, "chan"),
            P("chan"),
        ),
        out_specs=P(("clip", "tm"), "tile", "chan", None),
        check_vma=False,
    )
```

```python
import functools

import jax
import jax.numpy as jnp
from jax import lax
from jax.experimental import pallas as pl
from jax.experimental.pallas import tpu as pltpu
from jax.sharding import PartitionSpec as P

MESH = pl.DeviceIdType.MESH
C = 256
GROUPS = 32
SIZE = C // GROUPS
F32 = jnp.float32
BF16 = jnp.bfloat16


def iota(shape, dim):
    return lax.broadcasted_iota(jnp.int32, shape, dim)


def kernel(
    tiles,
    blocks,
    latent,
    n1g,
    n1b,
    w1,
    c1b,
    n2g,
    n2b,
    w2,
    c2b,
    out,
    raw,
    wv,
    lat,
    act1,
    act2,
    acc,
    hid,
    edge,
    halo,
    mix,
    select,
    params,
    own_stats,
    stats,
    gains,
    biases,
    part,
    landed,
    l_sem,
    own_sem,
    w_send,
    w_recv,
    x_send,
    x_recv,
    side_recv,
    r_recv,
    h_recv,
    s_recv,
    sent_a,
    sent_b,
):
    tm = lax.axis_index("tm")
    tile = lax.axis_index("tile")
    core = lax.axis_index("chan")
    other = 1 - core
    me = tm * tiles + tile
    rows, local, wide = latent.shape[1:]

    def where_is(index):
        return {"tm": index // tiles, "tile": index % tiles}

    def remote(src, dst, send, recv, **device):
        return pltpu.make_async_remote_copy(
            src_ref=src, dst_ref=dst, send_sem=send, recv_sem=recv, device_id=device, device_id_type=MESH
        )

    load = pltpu.make_async_copy(latent, raw, l_sem.at[0])
    load.start()
    barrier = pltpu.get_barrier_semaphore()

    earlier = (tm + 1) * tiles
    later = (blocks - tm) * tiles

    def greet(step, carry):
        pl.semaphore_signal(barrier, inc=1, device_id=where_is(lax.rem(me + step, earlier)), device_id_type=MESH)
        return carry

    lax.fori_loop(1, earlier, greet, 0)
    pl.semaphore_signal(barrier, inc=1, device_id={"chan": other}, device_id_type=MESH)
    param_loads = [
        pltpu.make_async_copy(ref, params.at[i], own_sem.at[0]) for i, ref in enumerate((n1g, n1b, n2g, n2b, c1b, c2b))
    ]
    for copy in param_loads:
        copy.start()

    def own_half(w, i):
        return pltpu.make_async_copy(
            w.at[:, pl.ds(pl.multiple_of(core * local, local), local)], wv.at[i, :, :, pl.ds(0, local)], own_sem.at[0]
        )

    def other_half(w, i):
        return remote(
            w.at[:, pl.ds(pl.multiple_of(other * local, local), local)], wv.at[i, :, :, pl.ds(local, local)],
            w_send.at[0], w_recv.at[i], chan=other,
        )

    own_half(w1, 0).start()
    own_half(w2, 1).start()

    has_up = tile < tiles - 1
    has_down = tile > 0
    slots = [s for s in range(3) if blocks > 2 - s]
    before = [s for s in slots if s < 2]

    def put_stats(which, rows_of):
        for i, row in enumerate(rows_of):
            own_stats[which, i:i + 1] = row
            stats[which, me, i:i + 1] = row

    def sent_of(which):
        return (sent_a, sent_b)[which].at[0]

    def send_stats(which):
        def send(step, carry):
            to = tm * tiles + lax.rem(tile + step, later)
            remote(own_stats.at[which], stats.at[which, me], sent_of(which), s_recv.at[which], **where_is(to)).start()
            return carry

        lax.fori_loop(1, later, send, 0)

    def of_stats(which, n):
        some = stats.at[which, pl.ds(0, n)]
        return remote(some, some, sent_of(which), s_recv.at[which], chan=other)

    def wait_stats(which):
        for b in range(blocks):
            pl.when(tm == b)(lambda b=b: of_stats(which, (b + 1) * tiles - 1).wait_recv())

    def sent_stats(which):
        for b in range(blocks):
            pl.when(tm == b)(lambda b=b: of_stats(which, (blocks - b) * tiles - 1).wait_send())

    def group_sum(v):
        lane = iota(v.shape, 1) % SIZE
        total = v
        for step in range(1, SIZE):
            total = total + jnp.where(lane >= step, pltpu.roll(v, step, 1), 0.0)
            total = total + jnp.where(lane < SIZE - step, pltpu.roll(v, 128 - step, 1), 0.0)
        return total

    def make_norms(which, frames, gain, bias, shift):
        ahead = frames // 2 - 1
        e = iota((8, 128), 0)
        block = tm - ahead + e // 2
        odd = jnp.logical_and(block >= 0, e % 2 == 1)
        block = jnp.maximum(block, 0)
        total = jnp.zeros((8, 128), F32)
        square = jnp.zeros((8, 128), F32)
        for b in range(blocks):
            s = jnp.sum(stats[which, pl.ds(b * tiles, tiles)], axis=0)
            first = b <= block
            second = jnp.logical_or(b < block, jnp.logical_and(b == block, odd))
            total = total + jnp.where(first, s[0:1], 0.0) + jnp.where(second, s[1:2], 0.0)
            square = square + jnp.where(first, s[2:3], 0.0) + jnp.where(second, s[3:4], 0.0)
        number = (block * 2 + odd.astype(jnp.int32) + 1).astype(F32)
        count = number * float(rows * tiles * SIZE * wide)
        mean = group_sum(total) / count
        var = group_sum(square) / count - mean * mean
        scale = 1.0 / jnp.sqrt(var + 1e-06)
        g = scale * (0.5 * gain)
        gains[which] = g
        biases[which] = 0.5 * bias + (shift - mean) * g

    at = iota((wide, local), 0)

    def norm_into(act, row, e, v, which):
        half = v * gains[which, pl.ds(e, 1)] + biases[which, pl.ds(e, 1)]
        v = half + half * jnp.tanh(half)
        act[0, row, e] = jnp.where(at == 0, 0.0, pltpu.roll(v, 1, 0)).astype(BF16)
        act[1, row, e] = v.astype(BF16)
        act[2, row, e] = jnp.where(at == wide - 1, 0.0, pltpu.roll(v, wide - 1, 0)).astype(BF16)

    def clear_edges(act):
        for side, row in ((has_down, 0), (has_up, 3)):
            @pl.when(jnp.logical_not(side))
            def _(row=row):
                act[:, row] = jnp.zeros((3,) + act.shape[2:], BF16)

    def taps(act, w, o, first, rows_of, js):
        lhs = jnp.concatenate(
            [
                jnp.concatenate(
                    [act[k, row, jnp.maximum(o + f + i, first)] for row in rows_of for i in range(3) for k in range(3)],
                    axis=1,
                )
                for f in range(2)
            ],
            axis=0,
        )
        rhs = jnp.concatenate([wv[w, 9 * i + 3 * j + k] for j in js for i in range(3) for k in range(3)], axis=0)
        return jnp.dot(lhs, rhs, preferred_element_type=F32)

    load.wait()
    sums = []
    for f in range(2):
        total = jnp.zeros((wide, local), F32)
        square = jnp.zeros((wide, local), F32)
        for r in range(2):
            t = raw[f, r].T
            lat[2, 1 + r, f] = t
            v = t.astype(F32)
            total = total + v
            square = square + v * v
        sums.append((jnp.sum(total, axis=0, keepdims=True), jnp.sum(square, axis=0, keepdims=True)))
    put_stats(0, (sums[0][0], sums[1][0], sums[0][1], sums[1][1]))
    pl.semaphore_wait(barrier, later)

    def lat_x(s, r, f):
        sem = sent_a.at[0] if f else x_send.at[s - slots[0]]
        return remote(
            lat.at[2, 1 + r, f], lat.at[s, 1 + r, f], sem, x_recv.at[s - slots[0], r, f], tm=tm + (2 - s)
        )

    def lat_side(at_s, s, r, f, **device):
        to, row = ((tile - 1, 3), (tile + 1, 0))[r]
        return remote(
            lat.at[at_s, 1 + r, f], lat.at[s, row, f], sent_a.at[0], side_recv.at[s - slots[0], 1 - r], tile=to, **device
        )

    def lat_z(s, r, f):
        return lat_side(s, s, r, f)

    def lat_xz(s, r, f):
        return lat_side(2, s, r, f, tm=tm + (2 - s))

    def side_of(r):
        return (has_down, has_up)[r]

    def send_x(s):
        for f in range(2):
            for r in range(2):
                lat_x(s, r, f).start()

    def send_xz(s):
        for r in range(2):
            @pl.when(side_of(r))
            def _(r=r):
                for f in range(2):
                    lat_xz(s, r, f).start()

    def pair_of(sem):
        pair = lat.at[2, 1]
        return remote(pair, pair, sem, side_recv.at[0, 0], chan=other)

    def sends_x(s):
        return tm + (2 - s) < blocks

    for s in reversed(before):
        pl.when(jnp.logical_and(sends_x(s), core == 0))(lambda s=s: send_x(s))

    send_stats(0)
    for r in range(2):
        @pl.when(side_of(r))
        def _(r=r):
            for f in range(2):
                lat_z(2, r, f).start()

    other_half(w1, 0).start()
    other_half(w2, 1).start()
    a, b = iota((2 * wide, 2 * wide), 0), iota((2 * wide, 2 * wide), 1)
    select[...] = jnp.where(b == 2 * (a % wide) + a // wide, 1.0, 0.0).astype(BF16)
    clear_edges(act1)
    clear_edges(act2)

    for s in reversed(before):
        pl.when(jnp.logical_and(sends_x(s), core == 1))(lambda s=s: send_x(s))

    for s in reversed(before):
        @pl.when(jnp.logical_and(sends_x(s), core == 0))
        def _(s=s):
            pair_of(x_send.at[s - slots[0]]).wait_send()
            send_xz(s)

    for s in reversed(before):
        @pl.when(tm >= 2 - s)
        def _(s=s):
            for f in range(2):
                for r in range(2):
                    lat_x(s, r, f).wait_recv()

                    @pl.when(jnp.logical_and(side_of(r), core == 1))
                    def _():
                        lat_z(s, r, f).start()

    for copy in param_loads:
        copy.wait()
    own_half(w1, 0).wait()
    own_half(w2, 1).wait()
    wait_stats(0)

    make_norms(0, 6, params[0], params[1], 0.0)

    def wait_side(s, r):
        pair = lat.at[s, (0, 3)[r]]
        remote(pair, pair, sent_a.at[0], side_recv.at[s - slots[0], r], chan=other).wait_recv()

    def norm1(s, rows_of):
        def one(f, carry):
            for row in rows_of:
                norm_into(act1, row, 2 * s + f, lat[s, row, f].astype(F32), 0)
            return carry

        lax.fori_loop(0, 2, one, 0)

    first1 = 4 - 2 * jnp.minimum(tm, 2)
    first2 = 2 - 2 * jnp.minimum(tm, 1)
    pairs = 1 + jnp.minimum(tm, 1)

    def norm1_sides(s):
        for r in range(2):
            @pl.when(side_of(r))
            def _(r=r):
                wait_side(s, r)
                norm1(s, ((0, 3)[r],))

    norm1(2, (1, 2))
    for s in reversed(before):
        pl.when(tm >= 2 - s)(lambda s=s: norm1(s, (1, 2)))
    other_half(w1, 0).wait_recv()

    def inner(act, w, p, o, first):
        for r in range(2):
            acc[p, r] = taps(act, w, o, first, (1, 2), (1 - r, 2 - r))

    def outer(act, w, p, o, first, send, to):
        for r in range(2):
            res = acc[p, r] + taps(act, w, o, first, ((0, 3)[r],), (2 * r,))
            hid[to, r] = res[:, :local]
            part[to, r] = res[:, local:].astype(BF16)
        send()

    def swap(p):
        return remote(part.at[p], landed.at[p], sent_b.at[0], r_recv.at[p], chan=other)

    def edge_copy(r):
        to, side = ((tile - 1, 1), (tile + 1, 0))[r]
        return remote(edge.at[r], halo.at[side, 1], sent_b.at[0], h_recv.at[side], tile=to)

    def edge_next(r):
        to, side = ((tile - 1, 1), (tile + 1, 0))[r]
        return remote(edge.at[r], halo.at[side, 0], sent_b.at[0], h_recv.at[side], tm=tm + 1, tile=to)

    def whole(p, r):
        h = hid[p, r] + landed[p, r].astype(F32)
        hid[p, r] = h
        return h + params[4]

    def own_frames():
        swap(1).wait_recv()
        both = [whole(1, r) for r in range(2)]
        total = both[0] + both[1]
        square = both[0] * both[0] + both[1] * both[1]
        frames_of = [slice(f * wide, (f + 1) * wide) for f in range(2)]
        put_stats(1, [jnp.sum(v[at_frame], axis=0, keepdims=True) for v in (total, square) for at_frame in frames_of])
        send_stats(1)
        for r in range(2):
            edge[r] = hid[1, r].astype(BF16)
            pl.when(jnp.logical_and(side_of(r), sends_x(1)))(lambda r=r: edge_next(r).start())
            pl.when(side_of(r))(lambda r=r: edge_copy(r).start())

    steps = 2 * pairs
    waits_long = jnp.logical_and(jnp.logical_and(has_up, has_down), tm >= 1).astype(jnp.int32)
    inner_last = 2 - waits_long
    outer_first = 1 + waits_long
    sum_step = jnp.where(core == 0, outer_first, steps - 1)

    def conv1(step, carry):
        is_inner = jnp.logical_or(step == 0, jnp.logical_and(step == inner_last, pairs == 2))

        @pl.when(is_inner)
        def _():
            p = jnp.where(step == 0, 1, 0)
            inner(act1, 0, p, 2 * p, first1)

        @pl.when(step == outer_first)
        def _():
            norm1_sides(2)
            for s in reversed(before):
                pl.when(tm >= 2 - s)(lambda s=s: norm1_sides(s))

        @pl.when(jnp.logical_not(is_inner))
        def _():
            p = jnp.where(step == outer_first, 1, 0)
            outer(act1, 0, p, 2 * p, first1, lambda: swap(p).start(), p)

        pl.when(step == sum_step)(own_frames)
        return carry

    lax.fori_loop(0, steps, conv1, 0)

    @pl.when(tm >= 1)
    def _():
        swap(0).wait_recv()
        for r in range(2):
            whole(0, r)

    def sent():
        sent_stats(0)
        for s in before:
            @pl.when(sends_x(s))
            def _(s=s):
                pair_of(sent_a.at[0]).wait_send()
                pl.when(core == 1)(lambda: pair_of(x_send.at[s - slots[0]]).wait_send())

        for s in slots:
            sends = core >= 0 if s == 2 else jnp.where(core == 1, tm >= 2 - s, sends_x(s))
            for r in range(2):
                pl.when(jnp.logical_and(side_of(r), sends))(lambda: pair_of(sent_a.at[0]).wait_send())

        half = wv.at[:, :, :, pl.ds(0, local)]
        remote(half, half, w_send.at[0], w_recv.at[0], chan=other).wait_send()

    sent()
    other_half(w2, 1).wait_recv()
    wait_stats(1)
    make_norms(1, 4, params[2], params[3], params[4])

    def norm2(p, carry):
        for f in range(2):
            for r in range(2):
                norm_into(act2, 1 + r, 2 * p + f, hid[p, r, f * wide:(f + 1) * wide], 1)
        return carry

    def wait_halo(side):
        for later_block, some in ((False, halo.at[side, 1]), (True, halo.at[side])):
            @pl.when((tm >= 1) == later_block)
            def _(some=some):
                remote(some, some, sent_b.at[0], h_recv.at[side], chan=other).wait_recv()

    def norms2(p):
        for side in range(2):
            @pl.when((has_down, has_up)[side])
            def _(side=side):
                for f in range(2):
                    v = halo[side, p, f * wide:(f + 1) * wide].astype(F32)
                    norm_into(act2, (0, 3)[side], 2 * p + f, v, 1)

    def norms2_of(step, carry):
        norms2(1 - step)
        return carry

    lax.fori_loop(2 - pairs, 2, norm2, 0)
    inner(act2, 1, 0, 0, first2)
    for side in range(2):
        pl.when((has_down, has_up)[side])(lambda side=side: wait_halo(side))
    lax.fori_loop(0, pairs, norms2_of, 0)
    def last_swap(r):
        return remote(part.at[2, r], landed.at[2, r], sent_b.at[0], r_recv.at[2 + r], chan=other)

    def send_last():
        for r in range(2):
            last_swap(r).start()

    outer(act2, 1, 0, 0, first2, send_last, 2)

    spread = select[...]
    sent_stats(1)
    swap(1).wait_send()
    pl.when(tm >= 1)(lambda: swap(0).wait_send())
    for r in range(2):
        pl.when(side_of(r))(lambda r=r: edge_copy(r).wait_send())
        pl.when(jnp.logical_and(side_of(r), sends_x(1)))(lambda r=r: edge_next(r).wait_send())

    for r in range(2):
        last_swap(r).wait_recv()
        for f in range(2):
            at_frame = slice(f * wide, (f + 1) * wide)
            v = lat[2, 1 + r, f].astype(F32) + (hid[2, r, at_frame] + landed[2, r, at_frame].astype(F32) + params[5])
            mix[f * 2 + r] = v.T
            for p in range(2):
                pair = [mix[f * 2 + r, pl.ds(2 * p + q, local // 4, stride=4), :].astype(BF16) for q in range(2)]
                out[f, 2 * r + p] = jnp.dot(
                    jnp.concatenate(pair, axis=1), spread, preferred_element_type=F32
                ).astype(BF16)

    swap(2).wait_send()


def shards(tiles, blocks, latent, n1g, n1b, w1, c1b, n2g, n2b, w2, c2b):
    frames, rows, local, wide = latent.shape
    peers = tiles * blocks
    before = min(blocks - 1, 2)
    vmem = pl.BlockSpec(memory_space=pltpu.VMEM)
    hbm = pl.BlockSpec(memory_space=pl.ANY)
    dma = pltpu.SemaphoreType.DMA
    here = lambda v: pltpu.with_memory_space_constraint(v, pltpu.HBM)
    row = lambda v: here(v.reshape(1, local))
    flat = lambda v: here(v.reshape(27, C, local))
    return pl.pallas_call(
        functools.partial(kernel, tiles, blocks),
        out_shape=jax.ShapeDtypeStruct((frames, 2 * rows, local // 4, 2 * wide), BF16),
        in_specs=[hbm] * 9,
        out_specs=vmem,
        scratch_shapes=[
            pltpu.VMEM(latent.shape, BF16),
            pltpu.VMEM((2, 27, local, C), BF16),
            pltpu.VMEM((3, 4, 2, wide, local), BF16),
            pltpu.VMEM((3, 4, 6, wide, local), BF16),
            pltpu.VMEM((3, 4, 4, wide, local), BF16),
            pltpu.VMEM((2, 2, 2 * wide, C), F32),
            pltpu.VMEM((3, 2, 2 * wide, local), F32),
            pltpu.VMEM((2, 2 * wide, local), BF16),
            pltpu.VMEM((2, 2, 2 * wide, local), BF16),
            pltpu.VMEM((4, local, wide), F32),
            pltpu.VMEM((2 * wide, 2 * wide), BF16),
            pltpu.VMEM((6, 1, local), F32),
            pltpu.VMEM((2, 4, local), F32),
            pltpu.VMEM((2, peers, 4, local), F32),
            pltpu.VMEM((2, 8, local), F32),
            pltpu.VMEM((2, 8, local), F32),
            pltpu.VMEM((3, 2, 2 * wide, local), BF16),
            pltpu.VMEM((3, 2, 2 * wide, local), BF16),
            dma((1,)),
            dma((1,)),
            dma((1,)),
            dma((2,)),
            dma((before,)),
            dma((before, 2, 2)),
            dma((before + 1, 2)),
            dma((4,)),
            dma((2,)),
            dma((2,)),
            dma((1,)),
            dma((1,)),
        ],
        compiler_params=pltpu.CompilerParams(
            collective_id=0, has_side_effects=True, vmem_limit_bytes=48 * 1024 * 1024
        ),
        name="block",
    )(here(latent), row(n1g), row(n1b), flat(w1), row(c1b), row(n2g), row(n2b), flat(w2), row(c2b))


def solution(mesh):
    return jax.shard_map(
        functools.partial(shards, mesh.shape["tile"], mesh.shape["tm"]),
        mesh=mesh,
        in_specs=(
            P(("clip", "tm"), "tile", "chan", None),
            P("chan"),
            P("chan"),
            P(None, None, None, None, "chan"),
            P("chan"),
            P("chan"),
            P("chan"),
            P(None, None, None, None, "chan"),
            P("chan"),
        ),
        out_specs=P(("clip", "tm"), "tile", "chan", None),
        check_vma=False,
    )
```

```python
import functools

import jax
import jax.numpy as jnp
from jax import lax
from jax.experimental import pallas as pl
from jax.experimental.pallas import tpu as pltpu
from jax.sharding import PartitionSpec as P

MESH = pl.DeviceIdType.MESH
C = 256
GROUPS = 32
SIZE = C // GROUPS
F32 = jnp.float32
BF16 = jnp.bfloat16


def iota(shape, dim):
    return lax.broadcasted_iota(jnp.int32, shape, dim)


def kernel(
    tiles,
    blocks,
    latent,
    n1g,
    n1b,
    w1,
    c1b,
    n2g,
    n2b,
    w2,
    c2b,
    out,
    raw,
    wv,
    lat,
    act1,
    act2,
    acc,
    hid,
    edge,
    halo,
    mix,
    select,
    params,
    own_stats,
    stats,
    gains,
    biases,
    part,
    landed,
    l_sem,
    own_sem,
    w_send,
    w_recv,
    x_send,
    x_recv,
    side_recv,
    r_recv,
    h_recv,
    s_recv,
    sent_a,
    sent_b,
):
    tm = lax.axis_index("tm")
    tile = lax.axis_index("tile")
    core = lax.axis_index("chan")
    other = 1 - core
    me = tm * tiles + tile
    rows, local, wide = latent.shape[1:]

    def where_is(index):
        return {"tm": index // tiles, "tile": index % tiles}

    def remote(src, dst, send, recv, **device):
        return pltpu.make_async_remote_copy(
            src_ref=src, dst_ref=dst, send_sem=send, recv_sem=recv, device_id=device, device_id_type=MESH
        )

    load = pltpu.make_async_copy(latent, raw, l_sem.at[0])
    load.start()
    barrier = pltpu.get_barrier_semaphore()

    earlier = (tm + 1) * tiles
    later = (blocks - tm) * tiles

    def greet(step, carry):
        pl.semaphore_signal(barrier, inc=1, device_id=where_is(lax.rem(me + step, earlier)), device_id_type=MESH)
        return carry

    lax.fori_loop(1, earlier, greet, 0)
    pl.semaphore_signal(barrier, inc=1, device_id={"chan": other}, device_id_type=MESH)
    param_loads = [
        pltpu.make_async_copy(ref, params.at[i], own_sem.at[0]) for i, ref in enumerate((n1g, n1b, n2g, n2b, c1b, c2b))
    ]
    for copy in param_loads:
        copy.start()

    def own_half(w, i):
        return pltpu.make_async_copy(
            w.at[:, pl.ds(pl.multiple_of(core * local, local), local)], wv.at[i, :, :, pl.ds(0, local)], own_sem.at[0]
        )

    def other_half(w, i):
        return remote(
            w.at[:, pl.ds(pl.multiple_of(other * local, local), local)], wv.at[i, :, :, pl.ds(local, local)],
            w_send.at[0], w_recv.at[i], chan=other,
        )

    own_half(w1, 0).start()
    own_half(w2, 1).start()

    has_up = tile < tiles - 1
    has_down = tile > 0
    slots = [s for s in range(3) if blocks > 2 - s]
    before = [s for s in slots if s < 2]

    def put_stats(which, rows_of):
        for i, row in enumerate(rows_of):
            own_stats[which, i:i + 1] = row
            stats[which, me, i:i + 1] = row

    def sent_of(which):
        return (sent_a, sent_b)[which].at[0]

    def send_stats(which):
        def send(step, carry):
            to = tm * tiles + lax.rem(tile + step, later)
            remote(own_stats.at[which], stats.at[which, me], sent_of(which), s_recv.at[which], **where_is(to)).start()
            return carry

        lax.fori_loop(1, later, send, 0)

    def of_stats(which, n):
        some = stats.at[which, pl.ds(0, n)]
        return remote(some, some, sent_of(which), s_recv.at[which], chan=other)

    def wait_stats(which):
        for b in range(blocks):
            pl.when(tm == b)(lambda b=b: of_stats(which, (b + 1) * tiles - 1).wait_recv())

    def sent_stats(which):
        for b in range(blocks):
            pl.when(tm == b)(lambda b=b: of_stats(which, (blocks - b) * tiles - 1).wait_send())

    def group_sum(v):
        lane = iota(v.shape, 1) % SIZE
        total = v
        for step in range(1, SIZE):
            total = total + jnp.where(lane >= step, pltpu.roll(v, step, 1), 0.0)
            total = total + jnp.where(lane < SIZE - step, pltpu.roll(v, 128 - step, 1), 0.0)
        return total

    def make_norms(which, frames, gain, bias, shift):
        ahead = frames // 2 - 1
        e = iota((8, 128), 0)
        block = tm - ahead + e // 2
        odd = jnp.logical_and(block >= 0, e % 2 == 1)
        block = jnp.maximum(block, 0)
        total = jnp.zeros((8, 128), F32)
        square = jnp.zeros((8, 128), F32)
        for b in range(blocks):
            s = jnp.sum(stats[which, pl.ds(b * tiles, tiles)], axis=0)
            first = b <= block
            second = jnp.logical_or(b < block, jnp.logical_and(b == block, odd))
            total = total + jnp.where(first, s[0:1], 0.0) + jnp.where(second, s[1:2], 0.0)
            square = square + jnp.where(first, s[2:3], 0.0) + jnp.where(second, s[3:4], 0.0)
        number = (block * 2 + odd.astype(jnp.int32) + 1).astype(F32)
        count = number * float(rows * tiles * SIZE * wide)
        mean = group_sum(total) / count
        var = group_sum(square) / count - mean * mean
        scale = 1.0 / jnp.sqrt(var + 1e-06)
        g = scale * (0.5 * gain)
        gains[which] = g
        biases[which] = 0.5 * bias + (shift - mean) * g

    at = iota((wide, local), 0)

    def norm_into(act, row, e, v, which):
        half = v * gains[which, pl.ds(e, 1)] + biases[which, pl.ds(e, 1)]
        v = half + half * jnp.tanh(half)
        act[0, row, e] = jnp.where(at == 0, 0.0, pltpu.roll(v, 1, 0)).astype(BF16)
        act[1, row, e] = v.astype(BF16)
        act[2, row, e] = jnp.where(at == wide - 1, 0.0, pltpu.roll(v, wide - 1, 0)).astype(BF16)

    def clear_edges(act):
        for side, row in ((has_down, 0), (has_up, 3)):
            @pl.when(jnp.logical_not(side))
            def _(row=row):
                act[:, row] = jnp.zeros((3,) + act.shape[2:], BF16)

    def taps(act, w, o, first, rows_of, js):
        lhs = jnp.concatenate(
            [
                jnp.concatenate(
                    [act[k, row, jnp.maximum(o + f + i, first)] for row in rows_of for i in range(3) for k in range(3)],
                    axis=1,
                )
                for f in range(2)
            ],
            axis=0,
        )
        rhs = jnp.concatenate([wv[w, 9 * i + 3 * j + k] for j in js for i in range(3) for k in range(3)], axis=0)
        return jnp.dot(lhs, rhs, preferred_element_type=F32)

    load.wait()
    sums = []
    for f in range(2):
        total = jnp.zeros((wide, local), F32)
        square = jnp.zeros((wide, local), F32)
        for r in range(2):
            t = raw[f, r].T
            lat[2, 1 + r, f] = t
            v = t.astype(F32)
            total = total + v
            square = square + v * v
        sums.append((jnp.sum(total, axis=0, keepdims=True), jnp.sum(square, axis=0, keepdims=True)))
    put_stats(0, (sums[0][0], sums[1][0], sums[0][1], sums[1][1]))
    pl.semaphore_wait(barrier, later)

    middle_first = (1 - tile // ((tiles + 1) // 2), tile // ((tiles + 1) // 2))

    def lat_x(s, n, f):
        r = middle_first[n]
        sem = sent_a.at[0] if n else x_send.at[s - slots[0]]
        return remote(
            lat.at[2, 1 + r, f], lat.at[s, 1 + r, f], sem, x_recv.at[s - slots[0], r, f], tm=tm + (2 - s)
        )

    def lat_side(at_s, s, r, f, **device):
        return remote(
            lat.at[at_s, 1 + r, f], lat.at[s, 3 - 3 * r, f], sent_a.at[0],
            side_recv.at[s - slots[0], 1 - r], tile=tile - 1 + 2 * r, **device
        )

    def lat_z(s, r, f):
        return lat_side(s, s, r, f)

    def lat_xz(s, r, f):
        return lat_side(2, s, r, f, tm=tm + (2 - s))

    def side_of(r):
        return jnp.where(r == 0, tile, tiles - 1 - tile) > 0

    def send_x(s):
        for n in range(2):
            for f in range(2):
                lat_x(s, n, f).start()

    def send_xz(s):
        for r in middle_first:
            @pl.when(side_of(r))
            def _(r=r):
                for f in range(2):
                    lat_xz(s, r, f).start()

    def pair_of(sem):
        pair = lat.at[2, 1]
        return remote(pair, pair, sem, side_recv.at[0, 0], chan=other)

    def sends_x(s):
        return tm + (2 - s) < blocks

    send_stats(0)
    for s in reversed(before):
        pl.when(jnp.logical_and(sends_x(s), core == 0))(lambda s=s: send_x(s))

    for r in range(2):
        @pl.when(side_of(r))
        def _(r=r):
            for f in range(2):
                lat_z(2, r, f).start()

    other_half(w1, 0).start()
    other_half(w2, 1).start()
    a, b = iota((2 * wide, 2 * wide), 0), iota((2 * wide, 2 * wide), 1)
    select[...] = jnp.where(b == 2 * (a % wide) + a // wide, 1.0, 0.0).astype(BF16)
    clear_edges(act1)
    clear_edges(act2)

    for s in reversed(before):
        pl.when(jnp.logical_and(sends_x(s), core == 1))(lambda s=s: send_x(s))

    for s in reversed(before):
        @pl.when(jnp.logical_and(sends_x(s), core == 0))
        def _(s=s):
            pair_of(x_send.at[s - slots[0]]).wait_send()
            send_xz(s)

    def rows_of_earlier(s):
        for n, r in enumerate(middle_first):
            for f in range(2):
                lat_x(s, n, f).wait_recv()

                @pl.when(jnp.logical_and(side_of(r), core == 1))
                def _():
                    lat_z(s, r, f).start()

    for s in reversed(before):
        pl.when(jnp.logical_and(tm >= 2 - s, core == 1))(lambda s=s: rows_of_earlier(s))

    for copy in param_loads:
        copy.wait()
    own_half(w1, 0).wait()
    own_half(w2, 1).wait()
    wait_stats(0)

    make_norms(0, 6, params[0], params[1], 0.0)

    def wait_side(s, r):
        pair = lat.at[s, (0, 3)[r]]
        remote(pair, pair, sent_a.at[0], side_recv.at[s - slots[0], r], chan=other).wait_recv()

    def norm1(s, rows_of):
        def one(f, carry):
            for row in rows_of:
                norm_into(act1, row, 2 * s + f, lat[s, row, f].astype(F32), 0)
            return carry

        lax.fori_loop(0, 2, one, 0)

    first1 = 4 - 2 * jnp.minimum(tm, 2)
    first2 = 2 - 2 * jnp.minimum(tm, 1)
    pairs = 1 + jnp.minimum(tm, 1)

    def norm1_sides(s):
        for r in range(2):
            @pl.when(side_of(r))
            def _(r=r):
                wait_side(s, r)
                norm1(s, ((0, 3)[r],))

    norm1(2, (1, 2))
    for s in reversed(before):
        @pl.when(tm >= 2 - s)
        def _(s=s):
            pl.when(core == 0)(lambda: rows_of_earlier(s))
            norm1(s, (1, 2))

    other_half(w1, 0).wait_recv()

    def inner(act, w, p, o, first):
        for r in range(2):
            acc[p, r] = taps(act, w, o, first, (1, 2), (1 - r, 2 - r))

    def split(to, r, res):
        hid[to, r] = res[:, :local]
        part[to, r] = res[:, local:].astype(BF16)

    def outer(act, w, p, o, first, send, to):
        for r in range(2):
            res = acc[p, r] + taps(act, w, o, first, ((0, 3)[r],), (2 * r,))
            split(to, r, res)
        send()

    def swap(p):
        return remote(part.at[p], landed.at[p], sent_b.at[0], r_recv.at[p], chan=other)

    def edge_copy(r):
        to, side = ((tile - 1, 1), (tile + 1, 0))[r]
        return remote(edge.at[r], halo.at[side, 1], sent_b.at[0], h_recv.at[side], tile=to)

    def edge_next(r):
        to, side = ((tile - 1, 1), (tile + 1, 0))[r]
        return remote(edge.at[r], halo.at[side, 0], sent_b.at[0], h_recv.at[side], tm=tm + 1, tile=to)

    def whole(p, r):
        h = hid[p, r] + landed[p, r].astype(F32)
        hid[p, r] = h
        return h + params[4]

    def own_frames():
        swap(1).wait_recv()
        both = [whole(1, r) for r in range(2)]
        total = both[0] + both[1]
        square = both[0] * both[0] + both[1] * both[1]
        frames_of = [slice(f * wide, (f + 1) * wide) for f in range(2)]
        put_stats(1, [jnp.sum(v[at_frame], axis=0, keepdims=True) for v in (total, square) for at_frame in frames_of])
        send_stats(1)
        for r in range(2):
            edge[r] = hid[1, r].astype(BF16)

        pl.when(side_of(0))(lambda: edge_copy(0).start())
        for r in range(2):
            pl.when(jnp.logical_and(side_of(r), sends_x(1)))(lambda r=r: edge_next(r).start())

        pl.when(side_of(1))(lambda: edge_copy(1).start())

    steps = 2 * pairs
    waits_long = jnp.logical_and(jnp.logical_and(has_up, has_down), tm >= 1).astype(jnp.int32)
    inner_last = 2 - waits_long
    outer_first = 1 + waits_long
    sum_step = jnp.where(core == 0, outer_first, steps - 1)

    def conv1(step, carry):
        is_inner = jnp.logical_or(step == 0, jnp.logical_and(step == inner_last, pairs == 2))

        @pl.when(is_inner)
        def _():
            p = jnp.where(step == 0, 1, 0)
            inner(act1, 0, p, 2 * p, first1)

        @pl.when(step == outer_first)
        def _():
            norm1_sides(2)
            for s in reversed(before):
                pl.when(tm >= 2 - s)(lambda s=s: norm1_sides(s))

        @pl.when(jnp.logical_not(is_inner))
        def _():
            p = jnp.where(step == outer_first, 1, 0)
            outer(act1, 0, p, 2 * p, first1, lambda: swap(p).start(), p)

        pl.when(step == sum_step)(own_frames)
        return carry

    lax.fori_loop(0, steps, conv1, 0)

    @pl.when(tm >= 1)
    def _():
        swap(0).wait_recv()
        for r in range(2):
            whole(0, r)

    def sent():
        sent_stats(0)
        for s in before:
            @pl.when(sends_x(s))
            def _(s=s):
                pair_of(sent_a.at[0]).wait_send()
                pl.when(core == 1)(lambda: pair_of(x_send.at[s - slots[0]]).wait_send())

        for s in slots:
            sends = core >= 0 if s == 2 else jnp.where(core == 1, tm >= 2 - s, sends_x(s))
            for r in range(2):
                pl.when(jnp.logical_and(side_of(r), sends))(lambda: pair_of(sent_a.at[0]).wait_send())

        half = wv.at[:, :, :, pl.ds(0, local)]
        remote(half, half, w_send.at[0], w_recv.at[0], chan=other).wait_send()

    sent()
    other_half(w2, 1).wait_recv()
    wait_stats(1)
    make_norms(1, 4, params[2], params[3], params[4])

    def norm2(p, carry):
        for f in range(2):
            for r in range(2):
                norm_into(act2, 1 + r, 2 * p + f, hid[p, r, f * wide:(f + 1) * wide], 1)
        return carry

    def wait_halo(side):
        for later_block, some in ((False, halo.at[side, 1]), (True, halo.at[side])):
            @pl.when((tm >= 1) == later_block)
            def _(some=some):
                remote(some, some, sent_b.at[0], h_recv.at[side], chan=other).wait_recv()

    def norms2(p):
        for side in range(2):
            @pl.when((has_down, has_up)[side])
            def _(side=side):
                for f in range(2):
                    v = halo[side, p, f * wide:(f + 1) * wide].astype(F32)
                    norm_into(act2, (0, 3)[side], 2 * p + f, v, 1)

    def norms2_of(step, carry):
        norms2(1 - step)
        return carry

    lax.fori_loop(2 - pairs, 2, norm2, 0)
    inner(act2, 1, 0, 0, first2)
    for side in range(2):
        pl.when((has_down, has_up)[side])(lambda side=side: wait_halo(side))
    lax.fori_loop(0, pairs, norms2_of, 0)
    def last_swap(r):
        return remote(part.at[2, r], landed.at[2, r], sent_b.at[0], r_recv.at[2 + r], chan=other)

    def send_last():
        for r in range(2):
            last_swap(r).start()

    outer(act2, 1, 0, 0, first2, send_last, 2)

    spread = select[...]
    sent_stats(1)
    swap(1).wait_send()
    pl.when(tm >= 1)(lambda: swap(0).wait_send())
    for r in range(2):
        pl.when(side_of(r))(lambda r=r: edge_copy(r).wait_send())
        pl.when(jnp.logical_and(side_of(r), sends_x(1)))(lambda r=r: edge_next(r).wait_send())

    for r in range(2):
        last_swap(r).wait_recv()
        for f in range(2):
            at_frame = slice(f * wide, (f + 1) * wide)
            v = lat[2, 1 + r, f].astype(F32) + (hid[2, r, at_frame] + landed[2, r, at_frame].astype(F32) + params[5])
            mix[f * 2 + r] = v.T
            for p in range(2):
                pair = [mix[f * 2 + r, pl.ds(2 * p + q, local // 4, stride=4), :].astype(BF16) for q in range(2)]
                out[f, 2 * r + p] = jnp.dot(
                    jnp.concatenate(pair, axis=1), spread, preferred_element_type=F32
                ).astype(BF16)

    swap(2).wait_send()


def shards(tiles, blocks, latent, n1g, n1b, w1, c1b, n2g, n2b, w2, c2b):
    frames, rows, local, wide = latent.shape
    peers = tiles * blocks
    before = min(blocks - 1, 2)
    vmem = pl.BlockSpec(memory_space=pltpu.VMEM)
    hbm = pl.BlockSpec(memory_space=pl.ANY)
    dma = pltpu.SemaphoreType.DMA
    here = lambda v: pltpu.with_memory_space_constraint(v, pltpu.HBM)
    row = lambda v: here(v.reshape(1, local))
    flat = lambda v: here(v.reshape(27, C, local))
    return pl.pallas_call(
        functools.partial(kernel, tiles, blocks),
        out_shape=jax.ShapeDtypeStruct((frames, 2 * rows, local // 4, 2 * wide), BF16),
        in_specs=[hbm] * 9,
        out_specs=vmem,
        scratch_shapes=[
            pltpu.VMEM(latent.shape, BF16),
            pltpu.VMEM((2, 27, local, C), BF16),
            pltpu.VMEM((3, 4, 2, wide, local), BF16),
            pltpu.VMEM((3, 4, 6, wide, local), BF16),
            pltpu.VMEM((3, 4, 4, wide, local), BF16),
            pltpu.VMEM((2, 2, 2 * wide, C), F32),
            pltpu.VMEM((3, 2, 2 * wide, local), F32),
            pltpu.VMEM((2, 2 * wide, local), BF16),
            pltpu.VMEM((2, 2, 2 * wide, local), BF16),
            pltpu.VMEM((4, local, wide), F32),
            pltpu.VMEM((2 * wide, 2 * wide), BF16),
            pltpu.VMEM((6, 1, local), F32),
            pltpu.VMEM((2, 4, local), F32),
            pltpu.VMEM((2, peers, 4, local), F32),
            pltpu.VMEM((2, 8, local), F32),
            pltpu.VMEM((2, 8, local), F32),
            pltpu.VMEM((3, 2, 2 * wide, local), BF16),
            pltpu.VMEM((3, 2, 2 * wide, local), BF16),
            dma((1,)),
            dma((1,)),
            dma((1,)),
            dma((2,)),
            dma((before,)),
            dma((before, 2, 2)),
            dma((before + 1, 2)),
            dma((4,)),
            dma((2,)),
            dma((2,)),
            dma((1,)),
            dma((1,)),
        ],
        compiler_params=pltpu.CompilerParams(
            collective_id=0, has_side_effects=True, vmem_limit_bytes=48 * 1024 * 1024
        ),
        name="block",
    )(here(latent), row(n1g), row(n1b), flat(w1), row(c1b), row(n2g), row(n2b), flat(w2), row(c2b))


def solution(mesh):
    return jax.shard_map(
        functools.partial(shards, mesh.shape["tile"], mesh.shape["tm"]),
        mesh=mesh,
        in_specs=(
            P(("clip", "tm"), "tile", "chan", None),
            P("chan"),
            P("chan"),
            P(None, None, None, None, "chan"),
            P("chan"),
            P("chan"),
            P("chan"),
            P(None, None, None, None, "chan"),
            P("chan"),
        ),
        out_specs=P(("clip", "tm"), "tile", "chan", None),
        check_vma=False,
    )
```

```python
import functools

import jax
import jax.numpy as jnp
from jax import lax
from jax.experimental import pallas as pl
from jax.experimental.pallas import tpu as pltpu
from jax.sharding import PartitionSpec as P

MESH = pl.DeviceIdType.MESH
C = 256
GROUPS = 32
SIZE = C // GROUPS
F32 = jnp.float32
BF16 = jnp.bfloat16


def iota(shape, dim):
    return lax.broadcasted_iota(jnp.int32, shape, dim)


def kernel(
    tiles,
    blocks,
    latent,
    n1g,
    n1b,
    w1,
    c1b,
    n2g,
    n2b,
    w2,
    c2b,
    out,
    raw,
    wv,
    lat,
    act1,
    act2,
    acc,
    hid,
    edge,
    halo,
    mix,
    select,
    params,
    own_stats,
    stats,
    gains,
    biases,
    part,
    landed,
    l_sem,
    own_sem,
    w_send,
    w_recv,
    x_send,
    x_recv,
    side_recv,
    r_recv,
    h_recv,
    s_recv,
    sent_a,
    sent_b,
):
    tm = lax.axis_index("tm")
    tile = lax.axis_index("tile")
    core = lax.axis_index("chan")
    other = 1 - core
    me = tm * tiles + tile
    rows, local, wide = latent.shape[1:]

    def where_is(index):
        return {"tm": index // tiles, "tile": index % tiles}

    def remote(src, dst, send, recv, **device):
        return pltpu.make_async_remote_copy(
            src_ref=src, dst_ref=dst, send_sem=send, recv_sem=recv, device_id=device, device_id_type=MESH
        )

    load = pltpu.make_async_copy(latent, raw, l_sem.at[0])
    load.start()
    barrier = pltpu.get_barrier_semaphore()

    earlier = (tm + 1) * tiles
    later = (blocks - tm) * tiles

    def greet(step, carry):
        pl.semaphore_signal(barrier, inc=1, device_id=where_is(lax.rem(me + step, earlier)), device_id_type=MESH)
        return carry

    lax.fori_loop(1, earlier, greet, 0)
    pl.semaphore_signal(barrier, inc=1, device_id={"chan": other}, device_id_type=MESH)
    param_loads = [
        pltpu.make_async_copy(ref, params.at[i], own_sem.at[0]) for i, ref in enumerate((n1g, n1b, n2g, n2b, c1b, c2b))
    ]
    for copy in param_loads:
        copy.start()

    def own_half(w, i):
        return pltpu.make_async_copy(
            w.at[:, pl.ds(pl.multiple_of(core * local, local), local)], wv.at[i, :, :, pl.ds(0, local)], own_sem.at[0]
        )

    def other_half(w, i):
        return remote(
            w.at[:, pl.ds(pl.multiple_of(other * local, local), local)], wv.at[i, :, :, pl.ds(local, local)],
            w_send.at[0], w_recv.at[i], chan=other,
        )

    own_half(w1, 0).start()
    own_half(w2, 1).start()

    has_up = tile < tiles - 1
    has_down = tile > 0
    slots = [s for s in range(3) if blocks > 2 - s]
    before = [s for s in slots if s < 2]

    def put_stats(which, rows_of):
        for i, row in enumerate(rows_of):
            own_stats[which, i:i + 1] = row
            stats[which, me, i:i + 1] = row

    def sent_of(which):
        return (sent_a, sent_b)[which].at[0]

    own_and_later = blocks - tm
    from_top = tile < tiles // 2

    def send_stats(which):
        def send(step, carry):
            n = step // own_and_later
            to = (tm + lax.rem(step, own_and_later)) * tiles + jnp.where(from_top, tiles - 1 - n, n)

            @pl.when(to != me)
            def _():
                remote(
                    own_stats.at[which], stats.at[which, me], sent_of(which), s_recv.at[which], **where_is(to)
                ).start()

            return carry

        lax.fori_loop(0, later, send, 0)

    def of_stats(which, n):
        some = stats.at[which, pl.ds(0, n)]
        return remote(some, some, sent_of(which), s_recv.at[which], chan=other)

    def wait_stats(which):
        for b in range(blocks):
            pl.when(tm == b)(lambda b=b: of_stats(which, (b + 1) * tiles - 1).wait_recv())

    def sent_stats(which):
        for b in range(blocks):
            pl.when(tm == b)(lambda b=b: of_stats(which, (blocks - b) * tiles - 1).wait_send())

    def group_sum(v):
        lane = iota(v.shape, 1) % SIZE
        total = v
        for step in range(1, SIZE):
            total = total + jnp.where(lane >= step, pltpu.roll(v, step, 1), 0.0)
            total = total + jnp.where(lane < SIZE - step, pltpu.roll(v, 128 - step, 1), 0.0)
        return total

    def make_norms(which, frames, gain, bias, shift):
        ahead = frames // 2 - 1
        e = iota((8, 128), 0)
        block = tm - ahead + e // 2
        odd = jnp.logical_and(block >= 0, e % 2 == 1)
        block = jnp.maximum(block, 0)
        total = jnp.zeros((8, 128), F32)
        square = jnp.zeros((8, 128), F32)
        for b in range(blocks):
            s = jnp.sum(stats[which, pl.ds(b * tiles, tiles)], axis=0)
            first = b <= block
            second = jnp.logical_or(b < block, jnp.logical_and(b == block, odd))
            total = total + jnp.where(first, s[0:1], 0.0) + jnp.where(second, s[1:2], 0.0)
            square = square + jnp.where(first, s[2:3], 0.0) + jnp.where(second, s[3:4], 0.0)
        number = (block * 2 + odd.astype(jnp.int32) + 1).astype(F32)
        count = number * float(rows * tiles * SIZE * wide)
        mean = group_sum(total) / count
        var = group_sum(square) / count - mean * mean
        scale = 1.0 / jnp.sqrt(var + 1e-06)
        g = scale * (0.5 * gain)
        gains[which] = g
        biases[which] = 0.5 * bias + (shift - mean) * g

    at = iota((wide, local), 0)

    def norm_into(act, row, e, v, which):
        half = v * gains[which, pl.ds(e, 1)] + biases[which, pl.ds(e, 1)]
        v = half + half * jnp.tanh(half)
        act[0, row, e] = jnp.where(at == 0, 0.0, pltpu.roll(v, 1, 0)).astype(BF16)
        act[1, row, e] = v.astype(BF16)
        act[2, row, e] = jnp.where(at == wide - 1, 0.0, pltpu.roll(v, wide - 1, 0)).astype(BF16)

    def clear_edges(act):
        for side, row in ((has_down, 0), (has_up, 3)):
            @pl.when(jnp.logical_not(side))
            def _(row=row):
                act[:, row] = jnp.zeros((3,) + act.shape[2:], BF16)

    def taps(act, w, o, first, rows_of, js):
        lhs = jnp.concatenate(
            [
                jnp.concatenate(
                    [act[k, row, jnp.maximum(o + f + i, first)] for row in rows_of for i in range(3) for k in range(3)],
                    axis=1,
                )
                for f in range(2)
            ],
            axis=0,
        )
        rhs = jnp.concatenate([wv[w, 9 * i + 3 * j + k] for j in js for i in range(3) for k in range(3)], axis=0)
        return jnp.dot(lhs, rhs, preferred_element_type=F32)

    load.wait()
    sums = []
    for f in range(2):
        total = jnp.zeros((wide, local), F32)
        square = jnp.zeros((wide, local), F32)
        for r in range(2):
            t = raw[f, r].T
            lat[2, 1 + r, f] = t
            v = t.astype(F32)
            total = total + v
            square = square + v * v
        sums.append((jnp.sum(total, axis=0, keepdims=True), jnp.sum(square, axis=0, keepdims=True)))
    put_stats(0, (sums[0][0], sums[1][0], sums[0][1], sums[1][1]))
    pl.semaphore_wait(barrier, later)

    middle_first = (1 - tile // ((tiles + 1) // 2), tile // ((tiles + 1) // 2))

    def lat_x(s, n, f):
        r = middle_first[n]
        sem = sent_a.at[0] if n else x_send.at[s - slots[0]]
        return remote(
            lat.at[2, 1 + r, f], lat.at[s, 1 + r, f], sem, x_recv.at[s - slots[0], r, f], tm=tm + (2 - s)
        )

    def lat_side(at_s, s, r, f, **device):
        return remote(
            lat.at[at_s, 1 + r, f], lat.at[s, 3 - 3 * r, f], sent_a.at[0],
            side_recv.at[s - slots[0], 1 - r], tile=tile - 1 + 2 * r, **device
        )

    def lat_z(s, r, f):
        return lat_side(s, s, r, f)

    def lat_xz(s, r, f):
        return lat_side(2, s, r, f, tm=tm + (2 - s))

    def side_of(r):
        return jnp.where(r == 0, tile, tiles - 1 - tile) > 0

    def send_x(s):
        for n in range(2):
            for f in range(2):
                lat_x(s, n, f).start()

    def send_xz(s):
        for r in middle_first:
            @pl.when(side_of(r))
            def _(r=r):
                for f in range(2):
                    lat_xz(s, r, f).start()

    def pair_of(sem):
        pair = lat.at[2, 1]
        return remote(pair, pair, sem, side_recv.at[0, 0], chan=other)

    def sends_x(s):
        return tm + (2 - s) < blocks

    send_stats(0)
    for s in reversed(before):
        pl.when(jnp.logical_and(sends_x(s), core == 0))(lambda s=s: send_x(s))

    for r in range(2):
        @pl.when(side_of(r))
        def _(r=r):
            for f in range(2):
                lat_z(2, r, f).start()

    other_half(w1, 0).start()
    other_half(w2, 1).start()
    a, b = iota((2 * wide, 2 * wide), 0), iota((2 * wide, 2 * wide), 1)
    select[...] = jnp.where(b == 2 * (a % wide) + a // wide, 1.0, 0.0).astype(BF16)
    clear_edges(act1)
    clear_edges(act2)

    for s in reversed(before):
        pl.when(jnp.logical_and(sends_x(s), core == 1))(lambda s=s: send_x(s))

    for s in reversed(before):
        @pl.when(jnp.logical_and(sends_x(s), core == 0))
        def _(s=s):
            pair_of(x_send.at[s - slots[0]]).wait_send()
            send_xz(s)

    def rows_of_earlier(s):
        for n, r in enumerate(middle_first):
            for f in range(2):
                lat_x(s, n, f).wait_recv()

                @pl.when(jnp.logical_and(side_of(r), core == 1))
                def _():
                    lat_z(s, r, f).start()

    for s in reversed(before):
        pl.when(jnp.logical_and(tm >= 2 - s, core == 1))(lambda s=s: rows_of_earlier(s))

    for copy in param_loads:
        copy.wait()
    own_half(w1, 0).wait()
    own_half(w2, 1).wait()
    wait_stats(0)

    make_norms(0, 6, params[0], params[1], 0.0)

    def wait_side(s, r):
        pair = lat.at[s, (0, 3)[r]]
        remote(pair, pair, sent_a.at[0], side_recv.at[s - slots[0], r], chan=other).wait_recv()

    def norm1(s, rows_of):
        def one(f, carry):
            for row in rows_of:
                norm_into(act1, row, 2 * s + f, lat[s, row, f].astype(F32), 0)
            return carry

        lax.fori_loop(0, 2, one, 0)

    first1 = 4 - 2 * jnp.minimum(tm, 2)
    first2 = 2 - 2 * jnp.minimum(tm, 1)
    pairs = 1 + jnp.minimum(tm, 1)

    def norm1_sides(s):
        for r in range(2):
            @pl.when(side_of(r))
            def _(r=r):
                wait_side(s, r)
                norm1(s, ((0, 3)[r],))

    norm1(2, (1, 2))
    for s in reversed(before):
        @pl.when(tm >= 2 - s)
        def _(s=s):
            pl.when(core == 0)(lambda: rows_of_earlier(s))
            norm1(s, (1, 2))

    other_half(w1, 0).wait_recv()

    def inner(act, w, p, o, first):
        for r in range(2):
            acc[p, r] = taps(act, w, o, first, (1, 2), (1 - r, 2 - r))

    def split(to, r, res):
        hid[to, r] = res[:, :local]
        part[to, r] = res[:, local:].astype(BF16)

    def outer(act, w, p, o, first, send, to):
        for r in range(2):
            res = acc[p, r] + taps(act, w, o, first, ((0, 3)[r],), (2 * r,))
            split(to, r, res)
        send()

    def swap(p):
        return remote(part.at[p], landed.at[p], sent_b.at[0], r_recv.at[p], chan=other)

    def edge_copy(r):
        to, side = ((tile - 1, 1), (tile + 1, 0))[r]
        return remote(edge.at[r], halo.at[side, 1], sent_b.at[0], h_recv.at[side], tile=to)

    def edge_next(r):
        to, side = ((tile - 1, 1), (tile + 1, 0))[r]
        return remote(edge.at[r], halo.at[side, 0], sent_b.at[0], h_recv.at[side], tm=tm + 1, tile=to)

    def whole(p, r):
        h = hid[p, r] + landed[p, r].astype(F32)
        hid[p, r] = h
        return h + params[4]

    def own_frames():
        swap(1).wait_recv()
        both = [whole(1, r) for r in range(2)]
        total = both[0] + both[1]
        square = both[0] * both[0] + both[1] * both[1]
        frames_of = [slice(f * wide, (f + 1) * wide) for f in range(2)]
        put_stats(1, [jnp.sum(v[at_frame], axis=0, keepdims=True) for v in (total, square) for at_frame in frames_of])
        send_stats(1)
        for r in range(2):
            edge[r] = hid[1, r].astype(BF16)

        pl.when(side_of(0))(lambda: edge_copy(0).start())
        for r in range(2):
            pl.when(jnp.logical_and(side_of(r), sends_x(1)))(lambda r=r: edge_next(r).start())

        pl.when(side_of(1))(lambda: edge_copy(1).start())

    steps = 2 * pairs
    waits_long = jnp.logical_and(jnp.logical_and(has_up, has_down), tm >= 1).astype(jnp.int32)
    inner_last = 2 - waits_long
    outer_first = 1 + waits_long
    sum_step = jnp.where(core == 0, outer_first, steps - 1)

    def conv1(step, carry):
        is_inner = jnp.logical_or(step == 0, jnp.logical_and(step == inner_last, pairs == 2))

        @pl.when(is_inner)
        def _():
            p = jnp.where(step == 0, 1, 0)
            inner(act1, 0, p, 2 * p, first1)

        @pl.when(step == outer_first)
        def _():
            norm1_sides(2)
            for s in reversed(before):
                pl.when(tm >= 2 - s)(lambda s=s: norm1_sides(s))

        @pl.when(jnp.logical_not(is_inner))
        def _():
            p = jnp.where(step == outer_first, 1, 0)
            outer(act1, 0, p, 2 * p, first1, lambda: swap(p).start(), p)

        pl.when(step == sum_step)(own_frames)
        return carry

    lax.fori_loop(0, steps, conv1, 0)

    @pl.when(tm >= 1)
    def _():
        swap(0).wait_recv()
        for r in range(2):
            whole(0, r)

    def sent():
        sent_stats(0)
        for s in before:
            @pl.when(sends_x(s))
            def _(s=s):
                pair_of(sent_a.at[0]).wait_send()
                pl.when(core == 1)(lambda: pair_of(x_send.at[s - slots[0]]).wait_send())

        for s in slots:
            sends = core >= 0 if s == 2 else jnp.where(core == 1, tm >= 2 - s, sends_x(s))
            for r in range(2):
                pl.when(jnp.logical_and(side_of(r), sends))(lambda: pair_of(sent_a.at[0]).wait_send())

        half = wv.at[:, :, :, pl.ds(0, local)]
        remote(half, half, w_send.at[0], w_recv.at[0], chan=other).wait_send()

    sent()
    other_half(w2, 1).wait_recv()
    wait_stats(1)
    make_norms(1, 4, params[2], params[3], params[4])

    def norm2(p, carry):
        for f in range(2):
            for r in range(2):
                norm_into(act2, 1 + r, 2 * p + f, hid[p, r, f * wide:(f + 1) * wide], 1)
        return carry

    def wait_halo(side):
        for later_block, some in ((False, halo.at[side, 1]), (True, halo.at[side])):
            @pl.when((tm >= 1) == later_block)
            def _(some=some):
                remote(some, some, sent_b.at[0], h_recv.at[side], chan=other).wait_recv()

    def norms2(p):
        for side in range(2):
            @pl.when((has_down, has_up)[side])
            def _(side=side):
                for f in range(2):
                    v = halo[side, p, f * wide:(f + 1) * wide].astype(F32)
                    norm_into(act2, (0, 3)[side], 2 * p + f, v, 1)

    def norms2_of(step, carry):
        norms2(1 - step)
        return carry

    lax.fori_loop(2 - pairs, 2, norm2, 0)
    inner(act2, 1, 0, 0, first2)
    for side in range(2):
        pl.when((has_down, has_up)[side])(lambda side=side: wait_halo(side))
    lax.fori_loop(0, pairs, norms2_of, 0)
    def last_swap(r):
        return remote(part.at[2, r], landed.at[2, r], sent_b.at[0], r_recv.at[2 + r], chan=other)

    def send_last():
        for r in range(2):
            last_swap(r).start()

    outer(act2, 1, 0, 0, first2, send_last, 2)

    spread = select[...]
    sent_stats(1)
    swap(1).wait_send()
    pl.when(tm >= 1)(lambda: swap(0).wait_send())
    for r in range(2):
        pl.when(side_of(r))(lambda r=r: edge_copy(r).wait_send())
        pl.when(jnp.logical_and(side_of(r), sends_x(1)))(lambda r=r: edge_next(r).wait_send())

    for r in range(2):
        last_swap(r).wait_recv()
        for f in range(2):
            at_frame = slice(f * wide, (f + 1) * wide)
            v = lat[2, 1 + r, f].astype(F32) + (hid[2, r, at_frame] + landed[2, r, at_frame].astype(F32) + params[5])
            mix[f * 2 + r] = v.T
            for p in range(2):
                pair = [mix[f * 2 + r, pl.ds(2 * p + q, local // 4, stride=4), :].astype(BF16) for q in range(2)]
                out[f, 2 * r + p] = jnp.dot(
                    jnp.concatenate(pair, axis=1), spread, preferred_element_type=F32
                ).astype(BF16)

    swap(2).wait_send()


def shards(tiles, blocks, latent, n1g, n1b, w1, c1b, n2g, n2b, w2, c2b):
    frames, rows, local, wide = latent.shape
    peers = tiles * blocks
    before = min(blocks - 1, 2)
    vmem = pl.BlockSpec(memory_space=pltpu.VMEM)
    hbm = pl.BlockSpec(memory_space=pl.ANY)
    dma = pltpu.SemaphoreType.DMA
    here = lambda v: pltpu.with_memory_space_constraint(v, pltpu.HBM)
    row = lambda v: here(v.reshape(1, local))
    flat = lambda v: here(v.reshape(27, C, local))
    return pl.pallas_call(
        functools.partial(kernel, tiles, blocks),
        out_shape=jax.ShapeDtypeStruct((frames, 2 * rows, local // 4, 2 * wide), BF16),
        in_specs=[hbm] * 9,
        out_specs=vmem,
        scratch_shapes=[
            pltpu.VMEM(latent.shape, BF16),
            pltpu.VMEM((2, 27, local, C), BF16),
            pltpu.VMEM((3, 4, 2, wide, local), BF16),
            pltpu.VMEM((3, 4, 6, wide, local), BF16),
            pltpu.VMEM((3, 4, 4, wide, local), BF16),
            pltpu.VMEM((2, 2, 2 * wide, C), F32),
            pltpu.VMEM((3, 2, 2 * wide, local), F32),
            pltpu.VMEM((2, 2 * wide, local), BF16),
            pltpu.VMEM((2, 2, 2 * wide, local), BF16),
            pltpu.VMEM((4, local, wide), F32),
            pltpu.VMEM((2 * wide, 2 * wide), BF16),
            pltpu.VMEM((6, 1, local), F32),
            pltpu.VMEM((2, 4, local), F32),
            pltpu.VMEM((2, peers, 4, local), F32),
            pltpu.VMEM((2, 8, local), F32),
            pltpu.VMEM((2, 8, local), F32),
            pltpu.VMEM((3, 2, 2 * wide, local), BF16),
            pltpu.VMEM((3, 2, 2 * wide, local), BF16),
            dma((1,)),
            dma((1,)),
            dma((1,)),
            dma((2,)),
            dma((before,)),
            dma((before, 2, 2)),
            dma((before + 1, 2)),
            dma((4,)),
            dma((2,)),
            dma((2,)),
            dma((1,)),
            dma((1,)),
        ],
        compiler_params=pltpu.CompilerParams(
            collective_id=0, has_side_effects=True, vmem_limit_bytes=48 * 1024 * 1024
        ),
        name="block",
    )(here(latent), row(n1g), row(n1b), flat(w1), row(c1b), row(n2g), row(n2b), flat(w2), row(c2b))


def solution(mesh):
    return jax.shard_map(
        functools.partial(shards, mesh.shape["tile"], mesh.shape["tm"]),
        mesh=mesh,
        in_specs=(
            P(("clip", "tm"), "tile", "chan", None),
            P("chan"),
            P("chan"),
            P(None, None, None, None, "chan"),
            P("chan"),
            P("chan"),
            P("chan"),
            P(None, None, None, None, "chan"),
            P("chan"),
        ),
        out_specs=P(("clip", "tm"), "tile", "chan", None),
        check_vma=False,
    )
```

```python
import functools

import jax
import jax.numpy as jnp
from jax import lax
from jax.experimental import pallas as pl
from jax.experimental.pallas import tpu as pltpu
from jax.sharding import PartitionSpec as P

MESH = pl.DeviceIdType.MESH
C = 256
GROUPS = 32
SIZE = C // GROUPS
F32 = jnp.float32
BF16 = jnp.bfloat16


def iota(shape, dim):
    return lax.broadcasted_iota(jnp.int32, shape, dim)


def kernel(
    tiles,
    blocks,
    latent,
    n1g,
    n1b,
    w1,
    c1b,
    n2g,
    n2b,
    w2,
    c2b,
    out,
    raw,
    wv,
    lat,
    act1,
    act2,
    acc,
    hid,
    edge,
    halo,
    mix,
    select,
    params,
    own_stats,
    stats,
    gains,
    biases,
    part,
    landed,
    l_sem,
    own_sem,
    w_send,
    w_recv,
    x_send,
    x_recv,
    side_recv,
    r_recv,
    h_recv,
    s_recv,
    sent_a,
    sent_b,
):
    tm = lax.axis_index("tm")
    tile = lax.axis_index("tile")
    core = lax.axis_index("chan")
    other = 1 - core
    me = tm * tiles + tile
    rows, local, wide = latent.shape[1:]

    def where_is(index):
        return {"tm": index // tiles, "tile": index % tiles}

    def remote(src, dst, send, recv, **device):
        return pltpu.make_async_remote_copy(
            src_ref=src, dst_ref=dst, send_sem=send, recv_sem=recv, device_id=device, device_id_type=MESH
        )

    load = pltpu.make_async_copy(latent, raw, l_sem.at[0])
    load.start()
    barrier = pltpu.get_barrier_semaphore()

    earlier = (tm + 1) * tiles
    later = (blocks - tm) * tiles

    def greet(step, carry):
        pl.semaphore_signal(barrier, inc=1, device_id=where_is(lax.rem(me + step, earlier)), device_id_type=MESH)
        return carry

    lax.fori_loop(1, earlier, greet, 0)
    pl.semaphore_signal(barrier, inc=1, device_id={"chan": other}, device_id_type=MESH)
    param_loads = [
        pltpu.make_async_copy(ref, params.at[i], own_sem.at[0]) for i, ref in enumerate((n1g, n1b, n2g, n2b, c1b, c2b))
    ]
    for copy in param_loads:
        copy.start()

    def own_half(w, i):
        return pltpu.make_async_copy(
            w.at[:, pl.ds(pl.multiple_of(core * local, local), local)], wv.at[i, :, :, pl.ds(0, local)], own_sem.at[0]
        )

    def other_half(w, i):
        return remote(
            w.at[:, pl.ds(pl.multiple_of(other * local, local), local)], wv.at[i, :, :, pl.ds(local, local)],
            w_send.at[0], w_recv.at[i], chan=other,
        )

    own_half(w1, 0).start()
    own_half(w2, 1).start()

    has_up = tile < tiles - 1
    has_down = tile > 0
    slots = [s for s in range(3) if blocks > 2 - s]
    before = [s for s in slots if s < 2]

    def put_stats(which, rows_of):
        for i, row in enumerate(rows_of):
            own_stats[which, i:i + 1] = row
            stats[which, me, i:i + 1] = row

    def sent_of(which):
        return (sent_a, sent_b)[which].at[0]

    own_and_later = blocks - tm
    from_top = tile < tiles // 2

    def send_stats(which):
        def send(step, carry):
            n = step // own_and_later
            to = (tm + lax.rem(step, own_and_later)) * tiles + jnp.where(from_top, tiles - 1 - n, n)

            @pl.when(to != me)
            def _():
                remote(
                    own_stats.at[which], stats.at[which, me], sent_of(which), s_recv.at[which], **where_is(to)
                ).start()

            return carry

        lax.fori_loop(0, later, send, 0)

    def of_stats(which, n):
        some = stats.at[which, pl.ds(0, n)]
        return remote(some, some, sent_of(which), s_recv.at[which], chan=other)

    def wait_stats(which):
        for b in range(blocks):
            pl.when(tm == b)(lambda b=b: of_stats(which, (b + 1) * tiles - 1).wait_recv())

    def sent_stats(which):
        for b in range(blocks):
            pl.when(tm == b)(lambda b=b: of_stats(which, (blocks - b) * tiles - 1).wait_send())

    def group_sum(v):
        lane = iota(v.shape, 1) % SIZE
        total = v
        for step in range(1, SIZE):
            total = total + jnp.where(lane >= step, pltpu.roll(v, step, 1), 0.0)
            total = total + jnp.where(lane < SIZE - step, pltpu.roll(v, 128 - step, 1), 0.0)
        return total

    def make_norms(which, frames, gain, bias, shift):
        ahead = frames // 2 - 1
        e = iota((8, 128), 0)
        block = tm - ahead + e // 2
        odd = jnp.logical_and(block >= 0, e % 2 == 1)
        block = jnp.maximum(block, 0)
        total = jnp.zeros((8, 128), F32)
        square = jnp.zeros((8, 128), F32)
        for b in range(blocks):
            s = jnp.sum(stats[which, pl.ds(b * tiles, tiles)], axis=0)
            first = b <= block
            second = jnp.logical_or(b < block, jnp.logical_and(b == block, odd))
            total = total + jnp.where(first, s[0:1], 0.0) + jnp.where(second, s[1:2], 0.0)
            square = square + jnp.where(first, s[2:3], 0.0) + jnp.where(second, s[3:4], 0.0)
        number = (block * 2 + odd.astype(jnp.int32) + 1).astype(F32)
        count = number * float(rows * tiles * SIZE * wide)
        mean = group_sum(total) / count
        var = group_sum(square) / count - mean * mean
        scale = 1.0 / jnp.sqrt(var + 1e-06)
        g = scale * (0.5 * gain)
        gains[which] = g
        biases[which] = 0.5 * bias + (shift - mean) * g

    at = iota((wide, local), 0)

    def norm_into(act, row, e, v, which):
        half = v * gains[which, pl.ds(e, 1)] + biases[which, pl.ds(e, 1)]
        v = half + half * jnp.tanh(half)
        act[0, row, e] = jnp.where(at == 0, 0.0, pltpu.roll(v, 1, 0)).astype(BF16)
        act[1, row, e] = v.astype(BF16)
        act[2, row, e] = jnp.where(at == wide - 1, 0.0, pltpu.roll(v, wide - 1, 0)).astype(BF16)

    def clear_edges(act):
        for side, row in ((has_down, 0), (has_up, 3)):
            @pl.when(jnp.logical_not(side))
            def _(row=row):
                act[:, row] = jnp.zeros((3,) + act.shape[2:], BF16)

    def taps(act, w, o, first, rows_of, js):
        lhs = jnp.concatenate(
            [
                jnp.concatenate(
                    [act[k, row, jnp.maximum(o + f + i, first)] for row in rows_of for i in range(3) for k in range(3)],
                    axis=1,
                )
                for f in range(2)
            ],
            axis=0,
        )
        rhs = jnp.concatenate([wv[w, 9 * i + 3 * j + k] for j in js for i in range(3) for k in range(3)], axis=0)
        return jnp.dot(lhs, rhs, preferred_element_type=F32)

    load.wait()
    sums = []
    for f in range(2):
        total = jnp.zeros((wide, local), F32)
        square = jnp.zeros((wide, local), F32)
        for r in range(2):
            t = raw[f, r].T
            lat[2, 1 + r, f] = t
            v = t.astype(F32)
            total = total + v
            square = square + v * v
        sums.append((jnp.sum(total, axis=0, keepdims=True), jnp.sum(square, axis=0, keepdims=True)))
    put_stats(0, (sums[0][0], sums[1][0], sums[0][1], sums[1][1]))
    pl.semaphore_wait(barrier, later)

    middle_first = (1 - tile // ((tiles + 1) // 2), tile // ((tiles + 1) // 2))

    def lat_x(s, n, f):
        r = middle_first[n]
        sem = sent_a.at[0] if n else x_send.at[s - slots[0]]
        return remote(
            lat.at[2, 1 + r, f], lat.at[s, 1 + r, f], sem, x_recv.at[s - slots[0], r, f], tm=tm + (2 - s)
        )

    def lat_side(at_s, s, r, f, **device):
        return remote(
            lat.at[at_s, 1 + r, f], lat.at[s, 3 - 3 * r, f], sent_a.at[0],
            side_recv.at[s - slots[0], 1 - r], tile=tile - 1 + 2 * r, **device
        )

    def lat_z(s, r, f):
        return lat_side(s, s, r, f)

    def lat_xz(s, r, f):
        return lat_side(2, s, r, f, tm=tm + (2 - s))

    def side_of(r):
        return jnp.where(r == 0, tile, tiles - 1 - tile) > 0

    def send_x(s):
        for n in range(2):
            for f in range(2):
                lat_x(s, n, f).start()

    def send_xz(s):
        for r in middle_first:
            @pl.when(side_of(r))
            def _(r=r):
                for f in range(2):
                    lat_xz(s, r, f).start()

    def pair_of(sem):
        pair = lat.at[2, 1]
        return remote(pair, pair, sem, side_recv.at[0, 0], chan=other)

    def sends_x(s):
        return tm + (2 - s) < blocks

    send_stats(0)
    for s in reversed(before):
        pl.when(jnp.logical_and(sends_x(s), core == 0))(lambda s=s: send_x(s))

    for r in range(2):
        @pl.when(side_of(r))
        def _(r=r):
            for f in range(2):
                lat_z(2, r, f).start()

    other_half(w1, 0).start()
    other_half(w2, 1).start()
    a, b = iota((2 * wide, 2 * wide), 0), iota((2 * wide, 2 * wide), 1)
    select[...] = jnp.where(b == 2 * (a % wide) + a // wide, 1.0, 0.0).astype(BF16)
    clear_edges(act1)
    clear_edges(act2)

    for s in reversed(before):
        pl.when(jnp.logical_and(sends_x(s), core == 1))(lambda s=s: send_x(s))

    for s in reversed(before):
        @pl.when(jnp.logical_and(sends_x(s), core == 0))
        def _(s=s):
            pair_of(x_send.at[s - slots[0]]).wait_send()
            send_xz(s)

    def rows_of_earlier(s):
        for n, r in enumerate(middle_first):
            for f in range(2):
                lat_x(s, n, f).wait_recv()

                @pl.when(jnp.logical_and(side_of(r), core == 1))
                def _():
                    lat_z(s, r, f).start()

    for s in reversed(before):
        pl.when(jnp.logical_and(tm >= 2 - s, core == 1))(lambda s=s: rows_of_earlier(s))

    for copy in param_loads:
        copy.wait()
    own_half(w1, 0).wait()
    own_half(w2, 1).wait()
    wait_stats(0)

    make_norms(0, 6, params[0], params[1], 0.0)

    def wait_side(s, r):
        pair = lat.at[s, (0, 3)[r]]
        remote(pair, pair, sent_a.at[0], side_recv.at[s - slots[0], r], chan=other).wait_recv()

    def norm1(s, rows_of):
        def one(f, carry):
            for row in rows_of:
                norm_into(act1, row, 2 * s + f, lat[s, row, f].astype(F32), 0)
            return carry

        lax.fori_loop(0, 2, one, 0)

    first1 = 4 - 2 * jnp.minimum(tm, 2)
    first2 = 2 - 2 * jnp.minimum(tm, 1)
    pairs = 1 + jnp.minimum(tm, 1)

    def norm1_sides(s):
        for r in range(2):
            @pl.when(side_of(r))
            def _(r=r):
                wait_side(s, r)
                norm1(s, ((0, 3)[r],))

    norm1(2, (1, 2))
    for s in reversed(before):
        @pl.when(tm >= 2 - s)
        def _(s=s):
            pl.when(core == 0)(lambda: rows_of_earlier(s))
            norm1(s, (1, 2))

    other_half(w1, 0).wait_recv()

    def inner(act, w, p, o, first):
        for r in range(2):
            acc[p, r] = taps(act, w, o, first, (1, 2), (1 - r, 2 - r))

    def split(to, r, res):
        hid[to, r] = res[:, :local]
        part[to, r] = res[:, local:].astype(BF16)

    def outer(act, w, p, o, first, send, to):
        for r in range(2):
            res = acc[p, r] + taps(act, w, o, first, ((0, 3)[r],), (2 * r,))
            split(to, r, res)
        send()

    def swap(p):
        return remote(part.at[p], landed.at[p], sent_b.at[0], r_recv.at[p], chan=other)

    def edge_copy(r):
        to, side = ((tile - 1, 1), (tile + 1, 0))[r]
        return remote(edge.at[r], halo.at[side, 1], sent_b.at[0], h_recv.at[side], tile=to)

    def edge_next(r):
        to, side = ((tile - 1, 1), (tile + 1, 0))[r]
        return remote(edge.at[r], halo.at[side, 0], sent_b.at[0], h_recv.at[side], tm=tm + 1, tile=to)

    def whole(p, r):
        h = hid[p, r] + landed[p, r].astype(F32)
        hid[p, r] = h
        return h + params[4]

    def own_frames():
        swap(1).wait_recv()
        both = [whole(1, r) for r in range(2)]
        total = both[0] + both[1]
        square = both[0] * both[0] + both[1] * both[1]
        frames_of = [slice(f * wide, (f + 1) * wide) for f in range(2)]
        put_stats(1, [jnp.sum(v[at_frame], axis=0, keepdims=True) for v in (total, square) for at_frame in frames_of])
        send_stats(1)
        for r in range(2):
            edge[r] = hid[1, r].astype(BF16)

        pl.when(side_of(0))(lambda: edge_copy(0).start())
        for r in range(2):
            pl.when(jnp.logical_and(side_of(r), sends_x(1)))(lambda r=r: edge_next(r).start())

        pl.when(side_of(1))(lambda: edge_copy(1).start())

    steps = 2 * pairs
    waits_long = jnp.logical_and(jnp.logical_and(has_up, has_down), tm >= 1).astype(jnp.int32)
    inner_last = 2 - waits_long
    outer_first = 1 + waits_long
    sum_step = jnp.where(core == 0, outer_first, steps - 1)

    def conv1(step, carry):
        is_inner = jnp.logical_and(pairs == 2, jnp.logical_or(step == 0, step == inner_last))

        @pl.when(is_inner)
        def _():
            p = jnp.where(step == 0, 1, 0)
            inner(act1, 0, p, 2 * p, first1)

        @pl.when(step == outer_first)
        def _():
            norm1_sides(2)
            for s in reversed(before):
                pl.when(tm >= 2 - s)(lambda s=s: norm1_sides(s))

        @pl.when(jnp.logical_and(pairs == 1, step == outer_first))
        def _():
            for r in range(2):
                split(1, r, taps(act1, 0, 2, first1, (r, r + 1, r + 2), (0, 1, 2)))
            swap(1).start()

        @pl.when(jnp.logical_and(pairs == 2, jnp.logical_not(is_inner)))
        def _():
            p = jnp.where(step == outer_first, 1, 0)
            outer(act1, 0, p, 2 * p, first1, lambda: swap(p).start(), p)

        pl.when(step == sum_step)(own_frames)
        return carry

    lax.fori_loop(0, steps, conv1, 0)

    @pl.when(tm >= 1)
    def _():
        swap(0).wait_recv()
        for r in range(2):
            whole(0, r)

    def sent():
        sent_stats(0)
        for s in before:
            @pl.when(sends_x(s))
            def _(s=s):
                pair_of(sent_a.at[0]).wait_send()
                pl.when(core == 1)(lambda: pair_of(x_send.at[s - slots[0]]).wait_send())

        for s in slots:
            sends = core >= 0 if s == 2 else jnp.where(core == 1, tm >= 2 - s, sends_x(s))
            for r in range(2):
                pl.when(jnp.logical_and(side_of(r), sends))(lambda: pair_of(sent_a.at[0]).wait_send())

        half = wv.at[:, :, :, pl.ds(0, local)]
        remote(half, half, w_send.at[0], w_recv.at[0], chan=other).wait_send()

    sent()
    other_half(w2, 1).wait_recv()
    wait_stats(1)
    make_norms(1, 4, params[2], params[3], params[4])

    def norm2(p, carry):
        for f in range(2):
            for r in range(2):
                norm_into(act2, 1 + r, 2 * p + f, hid[p, r, f * wide:(f + 1) * wide], 1)
        return carry

    def wait_halo(side):
        for later_block, some in ((False, halo.at[side, 1]), (True, halo.at[side])):
            @pl.when((tm >= 1) == later_block)
            def _(some=some):
                remote(some, some, sent_b.at[0], h_recv.at[side], chan=other).wait_recv()

    def norms2(p):
        for side in range(2):
            @pl.when((has_down, has_up)[side])
            def _(side=side):
                for f in range(2):
                    v = halo[side, p, f * wide:(f + 1) * wide].astype(F32)
                    norm_into(act2, (0, 3)[side], 2 * p + f, v, 1)

    def norms2_of(step, carry):
        norms2(1 - step)
        return carry

    lax.fori_loop(2 - pairs, 2, norm2, 0)
    inner(act2, 1, 0, 0, first2)
    for side in range(2):
        pl.when((has_down, has_up)[side])(lambda side=side: wait_halo(side))
    lax.fori_loop(0, pairs, norms2_of, 0)
    def last_swap(r):
        return remote(part.at[2, r], landed.at[2, r], sent_b.at[0], r_recv.at[2 + r], chan=other)

    def send_last():
        for r in range(2):
            last_swap(r).start()

    outer(act2, 1, 0, 0, first2, send_last, 2)

    spread = select[...]
    sent_stats(1)
    swap(1).wait_send()
    pl.when(tm >= 1)(lambda: swap(0).wait_send())
    for r in range(2):
        pl.when(side_of(r))(lambda r=r: edge_copy(r).wait_send())
        pl.when(jnp.logical_and(side_of(r), sends_x(1)))(lambda r=r: edge_next(r).wait_send())

    for r in range(2):
        last_swap(r).wait_recv()
        for f in range(2):
            at_frame = slice(f * wide, (f + 1) * wide)
            v = lat[2, 1 + r, f].astype(F32) + (hid[2, r, at_frame] + landed[2, r, at_frame].astype(F32) + params[5])
            mix[f * 2 + r] = v.T
            for p in range(2):
                pair = [mix[f * 2 + r, pl.ds(2 * p + q, local // 4, stride=4), :].astype(BF16) for q in range(2)]
                out[f, 2 * r + p] = jnp.dot(
                    jnp.concatenate(pair, axis=1), spread, preferred_element_type=F32
                ).astype(BF16)

    swap(2).wait_send()


def shards(tiles, blocks, latent, n1g, n1b, w1, c1b, n2g, n2b, w2, c2b):
    frames, rows, local, wide = latent.shape
    peers = tiles * blocks
    before = min(blocks - 1, 2)
    vmem = pl.BlockSpec(memory_space=pltpu.VMEM)
    hbm = pl.BlockSpec(memory_space=pl.ANY)
    dma = pltpu.SemaphoreType.DMA
    here = lambda v: pltpu.with_memory_space_constraint(v, pltpu.HBM)
    row = lambda v: here(v.reshape(1, local))
    flat = lambda v: here(v.reshape(27, C, local))
    return pl.pallas_call(
        functools.partial(kernel, tiles, blocks),
        out_shape=jax.ShapeDtypeStruct((frames, 2 * rows, local // 4, 2 * wide), BF16),
        in_specs=[hbm] * 9,
        out_specs=vmem,
        scratch_shapes=[
            pltpu.VMEM(latent.shape, BF16),
            pltpu.VMEM((2, 27, local, C), BF16),
            pltpu.VMEM((3, 4, 2, wide, local), BF16),
            pltpu.VMEM((3, 4, 6, wide, local), BF16),
            pltpu.VMEM((3, 4, 4, wide, local), BF16),
            pltpu.VMEM((2, 2, 2 * wide, C), F32),
            pltpu.VMEM((3, 2, 2 * wide, local), F32),
            pltpu.VMEM((2, 2 * wide, local), BF16),
            pltpu.VMEM((2, 2, 2 * wide, local), BF16),
            pltpu.VMEM((4, local, wide), F32),
            pltpu.VMEM((2 * wide, 2 * wide), BF16),
            pltpu.VMEM((6, 1, local), F32),
            pltpu.VMEM((2, 4, local), F32),
            pltpu.VMEM((2, peers, 4, local), F32),
            pltpu.VMEM((2, 8, local), F32),
            pltpu.VMEM((2, 8, local), F32),
            pltpu.VMEM((3, 2, 2 * wide, local), BF16),
            pltpu.VMEM((3, 2, 2 * wide, local), BF16),
            dma((1,)),
            dma((1,)),
            dma((1,)),
            dma((2,)),
            dma((before,)),
            dma((before, 2, 2)),
            dma((before + 1, 2)),
            dma((4,)),
            dma((2,)),
            dma((2,)),
            dma((1,)),
            dma((1,)),
        ],
        compiler_params=pltpu.CompilerParams(
            collective_id=0, has_side_effects=True, vmem_limit_bytes=48 * 1024 * 1024
        ),
        name="block",
    )(here(latent), row(n1g), row(n1b), flat(w1), row(c1b), row(n2g), row(n2b), flat(w2), row(c2b))


def solution(mesh):
    return jax.shard_map(
        functools.partial(shards, mesh.shape["tile"], mesh.shape["tm"]),
        mesh=mesh,
        in_specs=(
            P(("clip", "tm"), "tile", "chan", None),
            P("chan"),
            P("chan"),
            P(None, None, None, None, "chan"),
            P("chan"),
            P("chan"),
            P("chan"),
            P(None, None, None, None, "chan"),
            P("chan"),
        ),
        out_specs=P(("clip", "tm"), "tile", "chan", None),
        check_vma=False,
    )
```

```python
import functools

import jax
import jax.numpy as jnp
from jax import lax
from jax.experimental import pallas as pl
from jax.experimental.pallas import tpu as pltpu
from jax.sharding import PartitionSpec as P

MESH = pl.DeviceIdType.MESH
C = 256
GROUPS = 32
SIZE = C // GROUPS
F32 = jnp.float32
BF16 = jnp.bfloat16


def iota(shape, dim):
    return lax.broadcasted_iota(jnp.int32, shape, dim)


def kernel(
    tiles,
    blocks,
    latent,
    n1g,
    n1b,
    w1,
    c1b,
    n2g,
    n2b,
    w2,
    c2b,
    out,
    raw,
    wv,
    lat,
    act1,
    act2,
    acc,
    hid,
    edge,
    halo,
    mix,
    select,
    params,
    own_stats,
    stats,
    gains,
    biases,
    part,
    landed,
    l_sem,
    own_sem,
    w_send,
    w_recv,
    x_send,
    x_recv,
    side_recv,
    r_recv,
    h_recv,
    s_recv,
    sent_a,
    sent_b,
):
    tm = lax.axis_index("tm")
    tile = lax.axis_index("tile")
    core = lax.axis_index("chan")
    other = 1 - core
    me = tm * tiles + tile
    rows, local, wide = latent.shape[1:]

    def where_is(index):
        return {"tm": index // tiles, "tile": index % tiles}

    def remote(src, dst, send, recv, **device):
        return pltpu.make_async_remote_copy(
            src_ref=src, dst_ref=dst, send_sem=send, recv_sem=recv, device_id=device, device_id_type=MESH
        )

    load = pltpu.make_async_copy(latent, raw, l_sem.at[0])
    load.start()
    barrier = pltpu.get_barrier_semaphore()

    earlier = (tm + 1) * tiles
    later = (blocks - tm) * tiles

    def greet(step, carry):
        pl.semaphore_signal(barrier, inc=1, device_id=where_is(lax.rem(me + step, earlier)), device_id_type=MESH)
        return carry

    lax.fori_loop(1, earlier, greet, 0)
    pl.semaphore_signal(barrier, inc=1, device_id={"chan": other}, device_id_type=MESH)
    param_loads = [
        pltpu.make_async_copy(ref, params.at[i], own_sem.at[0]) for i, ref in enumerate((n1g, n1b, n2g, n2b, c1b, c2b))
    ]
    for copy in param_loads:
        copy.start()

    def own_half(w, i):
        return pltpu.make_async_copy(
            w.at[:, pl.ds(pl.multiple_of(core * local, local), local)], wv.at[i, :, :, pl.ds(0, local)], own_sem.at[0]
        )

    def other_half(w, i):
        return remote(
            w.at[:, pl.ds(pl.multiple_of(other * local, local), local)], wv.at[i, :, :, pl.ds(local, local)],
            w_send.at[0], w_recv.at[i], chan=other,
        )

    own_half(w1, 0).start()
    own_half(w2, 1).start()

    has_up = tile < tiles - 1
    has_down = tile > 0
    slots = [s for s in range(3) if blocks > 2 - s]
    before = [s for s in slots if s < 2]

    def put_stats(which, rows_of):
        for i, row in enumerate(rows_of):
            own_stats[which, i:i + 1] = row
            stats[which, me, i:i + 1] = row

    def sent_of(which):
        return (sent_a, sent_b)[which].at[0]

    own_and_later = blocks - tm
    from_top = tile < tiles // 2

    def send_stats(which):
        def send(step, carry):
            n = step // own_and_later
            to = (tm + lax.rem(step, own_and_later)) * tiles + jnp.where(from_top, tiles - 1 - n, n)

            @pl.when(to != me)
            def _():
                remote(
                    own_stats.at[which], stats.at[which, me], sent_of(which), s_recv.at[which], **where_is(to)
                ).start()

            return carry

        lax.fori_loop(0, later, send, 0)

    def of_stats(which, n):
        some = stats.at[which, pl.ds(0, n)]
        return remote(some, some, sent_of(which), s_recv.at[which], chan=other)

    def wait_stats(which):
        for b in range(blocks):
            pl.when(tm == b)(lambda b=b: of_stats(which, (b + 1) * tiles - 1).wait_recv())

    def sent_stats(which):
        for b in range(blocks):
            pl.when(tm == b)(lambda b=b: of_stats(which, (blocks - b) * tiles - 1).wait_send())

    def group_sum(v):
        lane = iota(v.shape, 1) % SIZE
        total = v
        for step in range(1, SIZE):
            total = total + jnp.where(lane >= step, pltpu.roll(v, step, 1), 0.0)
            total = total + jnp.where(lane < SIZE - step, pltpu.roll(v, 128 - step, 1), 0.0)
        return total

    def make_norms(which, frames, gain, bias, shift):
        ahead = frames // 2 - 1
        e = iota((8, 128), 0)
        block = tm - ahead + e // 2
        odd = jnp.logical_and(block >= 0, e % 2 == 1)
        block = jnp.maximum(block, 0)
        total = jnp.zeros((8, 128), F32)
        square = jnp.zeros((8, 128), F32)
        for b in range(blocks):
            s = jnp.sum(stats[which, pl.ds(b * tiles, tiles)], axis=0)
            first = b <= block
            second = jnp.logical_or(b < block, jnp.logical_and(b == block, odd))
            total = total + jnp.where(first, s[0:1], 0.0) + jnp.where(second, s[1:2], 0.0)
            square = square + jnp.where(first, s[2:3], 0.0) + jnp.where(second, s[3:4], 0.0)
        number = (block * 2 + odd.astype(jnp.int32) + 1).astype(F32)
        count = number * float(rows * tiles * SIZE * wide)
        mean = group_sum(total) / count
        var = group_sum(square) / count - mean * mean
        scale = 1.0 / jnp.sqrt(var + 1e-06)
        g = scale * (0.5 * gain)
        gains[which] = g
        biases[which] = 0.5 * bias + (shift - mean) * g

    at = iota((wide, local), 0)

    def norm_into(act, row, e, v, which):
        half = v * gains[which, pl.ds(e, 1)] + biases[which, pl.ds(e, 1)]
        v = half + half * jnp.tanh(half)
        act[0, row, e] = jnp.where(at == 0, 0.0, pltpu.roll(v, 1, 0)).astype(BF16)
        act[1, row, e] = v.astype(BF16)
        act[2, row, e] = jnp.where(at == wide - 1, 0.0, pltpu.roll(v, wide - 1, 0)).astype(BF16)

    def clear_edges(act):
        for side, row in ((has_down, 0), (has_up, 3)):
            @pl.when(jnp.logical_not(side))
            def _(row=row):
                act[:, row] = jnp.zeros((3,) + act.shape[2:], BF16)

    def taps(act, w, o, first, rows_of, js):
        lhs = jnp.concatenate(
            [
                jnp.concatenate(
                    [act[k, row, jnp.maximum(o + f + i, first)] for row in rows_of for i in range(3) for k in range(3)],
                    axis=1,
                )
                for f in range(2)
            ],
            axis=0,
        )
        rhs = jnp.concatenate([wv[w, 9 * i + 3 * j + k] for j in js for i in range(3) for k in range(3)], axis=0)
        return jnp.dot(lhs, rhs, preferred_element_type=F32)

    load.wait()
    sums = []
    for f in range(2):
        total = jnp.zeros((wide, local), F32)
        square = jnp.zeros((wide, local), F32)
        for r in range(2):
            t = raw[f, r].T
            lat[2, 1 + r, f] = t
            v = t.astype(F32)
            total = total + v
            square = square + v * v
        sums.append((jnp.sum(total, axis=0, keepdims=True), jnp.sum(square, axis=0, keepdims=True)))
    put_stats(0, (sums[0][0], sums[1][0], sums[0][1], sums[1][1]))
    pl.semaphore_wait(barrier, later)

    middle_first = (1 - tile // ((tiles + 1) // 2), tile // ((tiles + 1) // 2))

    def lat_x(s, n, f):
        r = middle_first[n]
        sem = sent_a.at[0] if n else x_send.at[s - slots[0]]
        return remote(
            lat.at[2, 1 + r, f], lat.at[s, 1 + r, f], sem, x_recv.at[s - slots[0], r, f], tm=tm + (2 - s)
        )

    def lat_side(at_s, s, r, f, **device):
        return remote(
            lat.at[at_s, 1 + r, f], lat.at[s, 3 - 3 * r, f], sent_a.at[0],
            side_recv.at[s - slots[0], 1 - r], tile=tile - 1 + 2 * r, **device
        )

    def lat_z(s, r, f):
        return lat_side(s, s, r, f)

    def lat_xz(s, r, f):
        return lat_side(2, s, r, f, tm=tm + (2 - s))

    def side_of(r):
        return jnp.where(r == 0, tile, tiles - 1 - tile) > 0

    def send_x(s):
        for n in range(2):
            for f in range(2):
                lat_x(s, n, f).start()

    def send_xz(s):
        for r in middle_first:
            @pl.when(side_of(r))
            def _(r=r):
                for f in range(2):
                    lat_xz(s, r, f).start()

    def pair_of(sem):
        pair = lat.at[2, 1]
        return remote(pair, pair, sem, side_recv.at[0, 0], chan=other)

    def sends_x(s):
        return tm + (2 - s) < blocks

    send_stats(0)
    for s in reversed(before):
        pl.when(jnp.logical_and(sends_x(s), core == 0))(lambda s=s: send_x(s))

    for r in range(2):
        @pl.when(side_of(r))
        def _(r=r):
            for f in range(2):
                lat_z(2, r, f).start()

    other_half(w1, 0).start()
    other_half(w2, 1).start()
    a, b = iota((2 * wide, 2 * wide), 0), iota((2 * wide, 2 * wide), 1)
    select[...] = jnp.where(b == 2 * (a % wide) + a // wide, 1.0, 0.0).astype(BF16)
    clear_edges(act1)
    clear_edges(act2)

    for s in reversed(before):
        pl.when(jnp.logical_and(sends_x(s), core == 1))(lambda s=s: send_x(s))

    for s in reversed(before):
        @pl.when(jnp.logical_and(sends_x(s), core == 0))
        def _(s=s):
            pair_of(x_send.at[s - slots[0]]).wait_send()
            send_xz(s)

    def rows_of_earlier(s):
        for n, r in enumerate(middle_first):
            for f in range(2):
                lat_x(s, n, f).wait_recv()

                @pl.when(jnp.logical_and(side_of(r), core == 1))
                def _():
                    lat_z(s, r, f).start()

    for s in reversed(before):
        pl.when(jnp.logical_and(tm >= 2 - s, core == 1))(lambda s=s: rows_of_earlier(s))

    for copy in param_loads:
        copy.wait()
    own_half(w1, 0).wait()
    own_half(w2, 1).wait()
    wait_stats(0)

    make_norms(0, 6, params[0], params[1], 0.0)

    def wait_side(s, r):
        pair = lat.at[s, (0, 3)[r]]
        remote(pair, pair, sent_a.at[0], side_recv.at[s - slots[0], r], chan=other).wait_recv()

    def norm1(s, rows_of):
        def one(f, carry):
            for row in rows_of:
                norm_into(act1, row, 2 * s + f, lat[s, row, f].astype(F32), 0)
            return carry

        lax.fori_loop(0, 2, one, 0)

    first1 = 4 - 2 * jnp.minimum(tm, 2)
    first2 = 2 - 2 * jnp.minimum(tm, 1)
    pairs = 1 + jnp.minimum(tm, 1)

    def norm1_sides(s):
        for r in range(2):
            @pl.when(side_of(r))
            def _(r=r):
                wait_side(s, r)
                norm1(s, ((0, 3)[r],))

    norm1(2, (1, 2))
    for s in reversed(before):
        @pl.when(tm >= 2 - s)
        def _(s=s):
            pl.when(core == 0)(lambda: rows_of_earlier(s))
            norm1(s, (1, 2))

    other_half(w1, 0).wait_recv()

    def inner(act, w, p, o, first):
        for r in range(2):
            acc[p, r] = taps(act, w, o, first, (1, 2), (1 - r, 2 - r))

    def split(to, r, res):
        hid[to, r] = res[:, :local]
        part[to, r] = res[:, local:].astype(BF16)

    def outer(act, w, p, o, first, send, to):
        for r in range(2):
            res = acc[p, r] + taps(act, w, o, first, ((0, 3)[r],), (2 * r,))
            split(to, r, res)
        send()

    def swap(p):
        return remote(part.at[p], landed.at[p], sent_b.at[0], r_recv.at[p], chan=other)

    def edge_copy(r):
        to, side = ((tile - 1, 1), (tile + 1, 0))[r]
        return remote(edge.at[r], halo.at[side, 1], sent_b.at[0], h_recv.at[side], tile=to)

    def edge_next(r):
        to, side = ((tile - 1, 1), (tile + 1, 0))[r]
        return remote(edge.at[r], halo.at[side, 0], sent_b.at[0], h_recv.at[side], tm=tm + 1, tile=to)

    def whole(p, r):
        h = hid[p, r] + landed[p, r].astype(F32)
        hid[p, r] = h
        return h + params[4]

    def own_frames():
        swap(1).wait_recv()
        both = [whole(1, r) for r in range(2)]
        total = both[0] + both[1]
        square = both[0] * both[0] + both[1] * both[1]
        frames_of = [slice(f * wide, (f + 1) * wide) for f in range(2)]
        put_stats(1, [jnp.sum(v[at_frame], axis=0, keepdims=True) for v in (total, square) for at_frame in frames_of])
        send_stats(1)
        for r in range(2):
            edge[r] = hid[1, r].astype(BF16)

        pl.when(side_of(0))(lambda: edge_copy(0).start())
        for r in range(2):
            pl.when(jnp.logical_and(side_of(r), sends_x(1)))(lambda r=r: edge_next(r).start())

        pl.when(side_of(1))(lambda: edge_copy(1).start())

    steps = 2 * pairs
    waits_long = jnp.logical_and(jnp.logical_and(has_up, has_down), tm >= 1).astype(jnp.int32)
    inner_last = 2 - waits_long
    outer_first = 1 + waits_long
    sum_step = jnp.where(core == 0, outer_first, steps - 1)

    def conv1(step, carry):
        is_inner = jnp.logical_or(step == 0, jnp.logical_and(step == inner_last, pairs == 2))

        @pl.when(is_inner)
        def _():
            p = jnp.where(step == 0, 1, 0)
            inner(act1, 0, p, 2 * p, first1)

        @pl.when(step == outer_first)
        def _():
            norm1_sides(2)
            for s in reversed(before):
                pl.when(tm >= 2 - s)(lambda s=s: norm1_sides(s))

        @pl.when(jnp.logical_not(is_inner))
        def _():
            p = jnp.where(step == outer_first, 1, 0)
            outer(act1, 0, p, 2 * p, first1, lambda: swap(p).start(), p)

        pl.when(step == sum_step)(own_frames)
        return carry

    lax.fori_loop(0, steps, conv1, 0)

    @pl.when(tm >= 1)
    def _():
        swap(0).wait_recv()
        for r in range(2):
            whole(0, r)

    def sent():
        sent_stats(0)
        for s in before:
            @pl.when(sends_x(s))
            def _(s=s):
                pair_of(sent_a.at[0]).wait_send()
                pl.when(core == 1)(lambda: pair_of(x_send.at[s - slots[0]]).wait_send())

        for s in slots:
            sends = core >= 0 if s == 2 else jnp.where(core == 1, tm >= 2 - s, sends_x(s))
            for r in range(2):
                pl.when(jnp.logical_and(side_of(r), sends))(lambda: pair_of(sent_a.at[0]).wait_send())

        half = wv.at[:, :, :, pl.ds(0, local)]
        remote(half, half, w_send.at[0], w_recv.at[0], chan=other).wait_send()

    sent()
    other_half(w2, 1).wait_recv()
    wait_stats(1)
    make_norms(1, 4, params[2], params[3], params[4])

    def norm2(p, carry):
        for f in range(2):
            for r in range(2):
                norm_into(act2, 1 + r, 2 * p + f, hid[p, r, f * wide:(f + 1) * wide], 1)
        return carry

    def wait_halo(side):
        for later_block, some in ((False, halo.at[side, 1]), (True, halo.at[side])):
            @pl.when((tm >= 1) == later_block)
            def _(some=some):
                remote(some, some, sent_b.at[0], h_recv.at[side], chan=other).wait_recv()

    def norms2(p):
        for side in range(2):
            @pl.when((has_down, has_up)[side])
            def _(side=side):
                for f in range(2):
                    v = halo[side, p, f * wide:(f + 1) * wide].astype(F32)
                    norm_into(act2, (0, 3)[side], 2 * p + f, v, 1)

    def norms2_of(step, carry):
        norms2(1 - step)
        return carry

    lax.fori_loop(2 - pairs, 2, norm2, 0)
    pl.when(tm > 0)(lambda: inner(act2, 1, 0, 0, first2))
    for side in range(2):
        pl.when((has_down, has_up)[side])(lambda side=side: wait_halo(side))
    lax.fori_loop(0, pairs, norms2_of, 0)
    def last_swap(r):
        return remote(part.at[2, r], landed.at[2, r], sent_b.at[0], r_recv.at[2 + r], chan=other)

    def send_last():
        for r in range(2):
            last_swap(r).start()

    pl.when(tm > 0)(lambda: outer(act2, 1, 0, 0, first2, send_last, 2))

    @pl.when(tm == 0)
    def _():
        for r in range(2):
            split(2, r, taps(act2, 1, 0, first2, (r, r + 1, r + 2), (0, 1, 2)))
        send_last()


    spread = select[...]
    sent_stats(1)
    swap(1).wait_send()
    pl.when(tm >= 1)(lambda: swap(0).wait_send())
    for r in range(2):
        pl.when(side_of(r))(lambda r=r: edge_copy(r).wait_send())
        pl.when(jnp.logical_and(side_of(r), sends_x(1)))(lambda r=r: edge_next(r).wait_send())

    for r in range(2):
        last_swap(r).wait_recv()
        for f in range(2):
            at_frame = slice(f * wide, (f + 1) * wide)
            v = lat[2, 1 + r, f].astype(F32) + (hid[2, r, at_frame] + landed[2, r, at_frame].astype(F32) + params[5])
            mix[f * 2 + r] = v.T
            for p in range(2):
                pair = [mix[f * 2 + r, pl.ds(2 * p + q, local // 4, stride=4), :].astype(BF16) for q in range(2)]
                out[f, 2 * r + p] = jnp.dot(
                    jnp.concatenate(pair, axis=1), spread, preferred_element_type=F32
                ).astype(BF16)

    swap(2).wait_send()


def shards(tiles, blocks, latent, n1g, n1b, w1, c1b, n2g, n2b, w2, c2b):
    frames, rows, local, wide = latent.shape
    peers = tiles * blocks
    before = min(blocks - 1, 2)
    vmem = pl.BlockSpec(memory_space=pltpu.VMEM)
    hbm = pl.BlockSpec(memory_space=pl.ANY)
    dma = pltpu.SemaphoreType.DMA
    here = lambda v: pltpu.with_memory_space_constraint(v, pltpu.HBM)
    row = lambda v: here(v.reshape(1, local))
    flat = lambda v: here(v.reshape(27, C, local))
    return pl.pallas_call(
        functools.partial(kernel, tiles, blocks),
        out_shape=jax.ShapeDtypeStruct((frames, 2 * rows, local // 4, 2 * wide), BF16),
        in_specs=[hbm] * 9,
        out_specs=vmem,
        scratch_shapes=[
            pltpu.VMEM(latent.shape, BF16),
            pltpu.VMEM((2, 27, local, C), BF16),
            pltpu.VMEM((3, 4, 2, wide, local), BF16),
            pltpu.VMEM((3, 4, 6, wide, local), BF16),
            pltpu.VMEM((3, 4, 4, wide, local), BF16),
            pltpu.VMEM((2, 2, 2 * wide, C), F32),
            pltpu.VMEM((3, 2, 2 * wide, local), F32),
            pltpu.VMEM((2, 2 * wide, local), BF16),
            pltpu.VMEM((2, 2, 2 * wide, local), BF16),
            pltpu.VMEM((4, local, wide), F32),
            pltpu.VMEM((2 * wide, 2 * wide), BF16),
            pltpu.VMEM((6, 1, local), F32),
            pltpu.VMEM((2, 4, local), F32),
            pltpu.VMEM((2, peers, 4, local), F32),
            pltpu.VMEM((2, 8, local), F32),
            pltpu.VMEM((2, 8, local), F32),
            pltpu.VMEM((3, 2, 2 * wide, local), BF16),
            pltpu.VMEM((3, 2, 2 * wide, local), BF16),
            dma((1,)),
            dma((1,)),
            dma((1,)),
            dma((2,)),
            dma((before,)),
            dma((before, 2, 2)),
            dma((before + 1, 2)),
            dma((4,)),
            dma((2,)),
            dma((2,)),
            dma((1,)),
            dma((1,)),
        ],
        compiler_params=pltpu.CompilerParams(
            collective_id=0, has_side_effects=True, vmem_limit_bytes=48 * 1024 * 1024
        ),
        name="block",
    )(here(latent), row(n1g), row(n1b), flat(w1), row(c1b), row(n2g), row(n2b), flat(w2), row(c2b))


def solution(mesh):
    return jax.shard_map(
        functools.partial(shards, mesh.shape["tile"], mesh.shape["tm"]),
        mesh=mesh,
        in_specs=(
            P(("clip", "tm"), "tile", "chan", None),
            P("chan"),
            P("chan"),
            P(None, None, None, None, "chan"),
            P("chan"),
            P("chan"),
            P("chan"),
            P(None, None, None, None, "chan"),
            P("chan"),
        ),
        out_specs=P(("clip", "tm"), "tile", "chan", None),
        check_vma=False,
    )
```

```python
import functools

import jax
import jax.numpy as jnp
from jax import lax
from jax.experimental import pallas as pl
from jax.experimental.pallas import tpu as pltpu
from jax.sharding import PartitionSpec as P

MESH = pl.DeviceIdType.MESH
C = 256
GROUPS = 32
SIZE = C // GROUPS
F32 = jnp.float32
BF16 = jnp.bfloat16


def iota(shape, dim):
    return lax.broadcasted_iota(jnp.int32, shape, dim)


def kernel(
    tiles,
    blocks,
    latent,
    n1g,
    n1b,
    w1,
    c1b,
    n2g,
    n2b,
    w2,
    c2b,
    out,
    raw,
    wv,
    lat,
    act1,
    act2,
    acc,
    hid,
    edge,
    halo,
    mix,
    select,
    params,
    own_stats,
    stats,
    gains,
    biases,
    part,
    landed,
    l_sem,
    own_sem,
    w_send,
    w_recv,
    x_send,
    x_recv,
    side_recv,
    r_recv,
    h_recv,
    s_recv,
    sent_a,
    sent_b,
):
    tm = lax.axis_index("tm")
    tile = lax.axis_index("tile")
    core = lax.axis_index("chan")
    other = 1 - core
    me = tm * tiles + tile
    rows, local, wide = latent.shape[1:]

    def where_is(index):
        return {"tm": index // tiles, "tile": index % tiles}

    def remote(src, dst, send, recv, **device):
        return pltpu.make_async_remote_copy(
            src_ref=src, dst_ref=dst, send_sem=send, recv_sem=recv, device_id=device, device_id_type=MESH
        )

    load = pltpu.make_async_copy(latent, raw, l_sem.at[0])
    load.start()
    barrier = pltpu.get_barrier_semaphore()

    earlier = (tm + 1) * tiles
    later = (blocks - tm) * tiles

    def greet(step, carry):
        pl.semaphore_signal(barrier, inc=1, device_id=where_is(lax.rem(me + step, earlier)), device_id_type=MESH)
        return carry

    lax.fori_loop(1, earlier, greet, 0)
    pl.semaphore_signal(barrier, inc=1, device_id={"chan": other}, device_id_type=MESH)
    param_loads = [
        pltpu.make_async_copy(ref, params.at[i], own_sem.at[0]) for i, ref in enumerate((n1g, n1b, n2g, n2b, c1b, c2b))
    ]
    for copy in param_loads:
        copy.start()

    def own_half(w, i):
        return pltpu.make_async_copy(
            w.at[:, pl.ds(pl.multiple_of(core * local, local), local)], wv.at[i, :, :, pl.ds(0, local)], own_sem.at[0]
        )

    def other_half(w, i):
        return remote(
            w.at[:, pl.ds(pl.multiple_of(other * local, local), local)], wv.at[i, :, :, pl.ds(local, local)],
            w_send.at[0], w_recv.at[i], chan=other,
        )

    own_half(w1, 0).start()
    own_half(w2, 1).start()

    has_up = tile < tiles - 1
    has_down = tile > 0
    slots = [s for s in range(3) if blocks > 2 - s]
    before = [s for s in slots if s < 2]

    def put_stats(which, rows_of):
        for i, row in enumerate(rows_of):
            own_stats[which, i:i + 1] = row
            stats[which, me, i:i + 1] = row

    def sent_of(which):
        return (sent_a, sent_b)[which].at[0]

    own_and_later = blocks - tm
    from_top = tile < tiles // 2

    def send_stats(which):
        def send(step, carry):
            n = step // own_and_later
            to = (tm + lax.rem(step, own_and_later)) * tiles + jnp.where(from_top, tiles - 1 - n, n)

            @pl.when(to != me)
            def _():
                remote(
                    own_stats.at[which], stats.at[which, me], sent_of(which), s_recv.at[which], **where_is(to)
                ).start()

            return carry

        lax.fori_loop(0, later, send, 0)

    def of_stats(which, n):
        some = stats.at[which, pl.ds(0, n)]
        return remote(some, some, sent_of(which), s_recv.at[which], chan=other)

    def wait_stats(which):
        for b in range(blocks):
            pl.when(tm == b)(lambda b=b: of_stats(which, (b + 1) * tiles - 1).wait_recv())

    def sent_stats(which):
        for b in range(blocks):
            pl.when(tm == b)(lambda b=b: of_stats(which, (blocks - b) * tiles - 1).wait_send())

    def group_sum(v):
        lane = iota(v.shape, 1) % SIZE
        total = v
        for step in range(1, SIZE):
            total = total + jnp.where(lane >= step, pltpu.roll(v, step, 1), 0.0)
            total = total + jnp.where(lane < SIZE - step, pltpu.roll(v, 128 - step, 1), 0.0)
        return total

    def make_norms(which, frames, gain, bias, shift):
        ahead = frames // 2 - 1
        e = iota((8, 128), 0)
        block = tm - ahead + e // 2
        odd = jnp.logical_and(block >= 0, e % 2 == 1)
        block = jnp.maximum(block, 0)
        total = jnp.zeros((8, 128), F32)
        square = jnp.zeros((8, 128), F32)
        for b in range(blocks):
            s = jnp.sum(stats[which, pl.ds(b * tiles, tiles)], axis=0)
            first = b <= block
            second = jnp.logical_or(b < block, jnp.logical_and(b == block, odd))
            total = total + jnp.where(first, s[0:1], 0.0) + jnp.where(second, s[1:2], 0.0)
            square = square + jnp.where(first, s[2:3], 0.0) + jnp.where(second, s[3:4], 0.0)
        number = (block * 2 + odd.astype(jnp.int32) + 1).astype(F32)
        count = number * float(rows * tiles * SIZE * wide)
        mean = group_sum(total) / count
        var = group_sum(square) / count - mean * mean
        scale = 1.0 / jnp.sqrt(var + 1e-06)
        g = scale * (0.5 * gain)
        gains[which] = g
        biases[which] = 0.5 * bias + (shift - mean) * g

    at = iota((wide, local), 0)

    def norm_into(act, row, e, v, which):
        half = v * gains[which, pl.ds(e, 1)] + biases[which, pl.ds(e, 1)]
        v = half + half * jnp.tanh(half)
        act[0, row, e] = jnp.where(at == 0, 0.0, pltpu.roll(v, 1, 0)).astype(BF16)
        act[1, row, e] = v.astype(BF16)
        act[2, row, e] = jnp.where(at == wide - 1, 0.0, pltpu.roll(v, wide - 1, 0)).astype(BF16)

    def clear_edges(act):
        for side, row in ((has_down, 0), (has_up, 3)):
            @pl.when(jnp.logical_not(side))
            def _(row=row):
                act[:, row] = jnp.zeros((3,) + act.shape[2:], BF16)

    def taps(act, w, o, first, rows_of, js):
        lhs = jnp.concatenate(
            [
                jnp.concatenate(
                    [act[k, row, jnp.maximum(o + f + i, first)] for row in rows_of for i in range(3) for k in range(3)],
                    axis=1,
                )
                for f in range(2)
            ],
            axis=0,
        )
        rhs = jnp.concatenate([wv[w, 9 * i + 3 * j + k] for j in js for i in range(3) for k in range(3)], axis=0)
        return jnp.dot(lhs, rhs, preferred_element_type=F32)

    load.wait()
    sums = []
    for f in range(2):
        total = jnp.zeros((wide, local), F32)
        square = jnp.zeros((wide, local), F32)
        for r in range(2):
            t = raw[f, r].T
            lat[2, 1 + r, f] = t
            v = t.astype(F32)
            total = total + v
            square = square + v * v
        sums.append((jnp.sum(total, axis=0, keepdims=True), jnp.sum(square, axis=0, keepdims=True)))
    put_stats(0, (sums[0][0], sums[1][0], sums[0][1], sums[1][1]))
    pl.semaphore_wait(barrier, later)

    middle_first = (1 - tile // ((tiles + 1) // 2), tile // ((tiles + 1) // 2))

    def lat_x(s, n, f):
        r = middle_first[n]
        sem = sent_a.at[0] if n else x_send.at[s - slots[0]]
        return remote(
            lat.at[2, 1 + r, f], lat.at[s, 1 + r, f], sem, x_recv.at[s - slots[0], r, f], tm=tm + (2 - s)
        )

    def lat_side(at_s, s, r, f, **device):
        return remote(
            lat.at[at_s, 1 + r, f], lat.at[s, 3 - 3 * r, f], sent_a.at[0],
            side_recv.at[s - slots[0], 1 - r], tile=tile - 1 + 2 * r, **device
        )

    def lat_z(s, r, f):
        return lat_side(s, s, r, f)

    def lat_xz(s, r, f):
        return lat_side(2, s, r, f, tm=tm + (2 - s))

    def side_of(r):
        return jnp.where(r == 0, tile, tiles - 1 - tile) > 0

    def send_x(s):
        for n in range(2):
            for f in range(2):
                lat_x(s, n, f).start()

    def send_xz(s):
        for r in middle_first:
            @pl.when(side_of(r))
            def _(r=r):
                for f in range(2):
                    lat_xz(s, r, f).start()

    def pair_of(sem):
        pair = lat.at[2, 1]
        return remote(pair, pair, sem, side_recv.at[0, 0], chan=other)

    def sends_x(s):
        return tm + (2 - s) < blocks

    send_stats(0)
    for s in reversed(before):
        pl.when(jnp.logical_and(sends_x(s), core == 0))(lambda s=s: send_x(s))

    for r in range(2):
        @pl.when(side_of(r))
        def _(r=r):
            for f in range(2):
                lat_z(2, r, f).start()

    other_half(w1, 0).start()
    other_half(w2, 1).start()
    a, b = iota((2 * wide, 2 * wide), 0), iota((2 * wide, 2 * wide), 1)
    select[...] = jnp.where(b == 2 * (a % wide) + a // wide, 1.0, 0.0).astype(BF16)
    clear_edges(act1)
    clear_edges(act2)

    for s in reversed(before):
        pl.when(jnp.logical_and(sends_x(s), core == 1))(lambda s=s: send_x(s))

    for s in reversed(before):
        @pl.when(jnp.logical_and(sends_x(s), core == 0))
        def _(s=s):
            pair_of(x_send.at[s - slots[0]]).wait_send()
            send_xz(s)

    def rows_of_earlier(s):
        for n, r in enumerate(middle_first):
            for f in range(2):
                lat_x(s, n, f).wait_recv()

                @pl.when(jnp.logical_and(side_of(r), core == 1))
                def _():
                    lat_z(s, r, f).start()

    for s in reversed(before):
        pl.when(jnp.logical_and(tm >= 2 - s, core == 1))(lambda s=s: rows_of_earlier(s))

    for copy in param_loads:
        copy.wait()
    own_half(w1, 0).wait()
    own_half(w2, 1).wait()
    wait_stats(0)

    make_norms(0, 6, params[0], params[1], 0.0)

    def wait_side(s, r):
        pair = lat.at[s, (0, 3)[r]]
        remote(pair, pair, sent_a.at[0], side_recv.at[s - slots[0], r], chan=other).wait_recv()

    def norm1(s, rows_of):
        def one(f, carry):
            for row in rows_of:
                norm_into(act1, row, 2 * s + f, lat[s, row, f].astype(F32), 0)
            return carry

        lax.fori_loop(0, 2, one, 0)

    first1 = 4 - 2 * jnp.minimum(tm, 2)
    first2 = 2 - 2 * jnp.minimum(tm, 1)
    pairs = 1 + jnp.minimum(tm, 1)

    def norm1_sides(s):
        for r in range(2):
            @pl.when(side_of(r))
            def _(r=r):
                wait_side(s, r)
                norm1(s, ((0, 3)[r],))

    norm1(2, (1, 2))
    for s in reversed(before):
        @pl.when(tm >= 2 - s)
        def _(s=s):
            pl.when(core == 0)(lambda: rows_of_earlier(s))
            norm1(s, (1, 2))

    other_half(w1, 0).wait_recv()

    def inner(act, w, p, o, first):
        for r in range(2):
            acc[p, r] = taps(act, w, o, first, (1, 2), (1 - r, 2 - r))

    def split(to, r, res):
        hid[to, r] = res[:, :local]
        part[to, r] = res[:, local:].astype(BF16)

    def outer(act, w, p, o, first, send, to):
        for r in range(2):
            res = acc[p, r] + taps(act, w, o, first, ((0, 3)[r],), (2 * r,))
            split(to, r, res)
        send()

    def swap(p):
        return remote(part.at[p], landed.at[p], sent_b.at[0], r_recv.at[p], chan=other)

    def edge_copy(r):
        to, side = ((tile - 1, 1), (tile + 1, 0))[r]
        return remote(edge.at[r], halo.at[side, 1], sent_b.at[0], h_recv.at[side], tile=to)

    def edge_next(r):
        to, side = ((tile - 1, 1), (tile + 1, 0))[r]
        return remote(edge.at[r], halo.at[side, 0], sent_b.at[0], h_recv.at[side], tm=tm + 1, tile=to)

    def whole(p, r):
        h = hid[p, r] + landed[p, r].astype(F32)
        hid[p, r] = h
        return h + params[4]

    def own_frames():
        swap(1).wait_recv()
        both = [whole(1, r) for r in range(2)]
        total = both[0] + both[1]
        square = both[0] * both[0] + both[1] * both[1]
        frames_of = [slice(f * wide, (f + 1) * wide) for f in range(2)]
        put_stats(1, [jnp.sum(v[at_frame], axis=0, keepdims=True) for v in (total, square) for at_frame in frames_of])
        send_stats(1)
        for r in range(2):
            edge[r] = hid[1, r].astype(BF16)

        pl.when(side_of(0))(lambda: edge_copy(0).start())
        for r in range(2):
            pl.when(jnp.logical_and(side_of(r), sends_x(1)))(lambda r=r: edge_next(r).start())

        pl.when(side_of(1))(lambda: edge_copy(1).start())

    steps = 2 * pairs
    waits_long = jnp.logical_and(jnp.logical_and(has_up, has_down), tm >= 1).astype(jnp.int32)
    inner_last = 2 - waits_long
    outer_first = 1 + waits_long
    sum_step = jnp.where(core == 0, outer_first, steps - 1)

    def conv1(step, carry):
        is_inner = jnp.logical_or(step == 0, jnp.logical_and(step == inner_last, pairs == 2))

        @pl.when(is_inner)
        def _():
            p = jnp.where(step == 0, 1, 0)
            inner(act1, 0, p, 2 * p, first1)

        @pl.when(step == outer_first)
        def _():
            norm1_sides(2)
            for s in reversed(before):
                pl.when(tm >= 2 - s)(lambda s=s: norm1_sides(s))

        @pl.when(jnp.logical_not(is_inner))
        def _():
            p = jnp.where(step == outer_first, 1, 0)
            outer(act1, 0, p, 2 * p, first1, lambda: swap(p).start(), p)

        pl.when(step == sum_step)(own_frames)
        return carry

    lax.fori_loop(0, steps, conv1, 0)

    @pl.when(tm >= 1)
    def _():
        swap(0).wait_recv()
        for r in range(2):
            whole(0, r)

    def sent():
        sent_stats(0)
        for s in before:
            @pl.when(sends_x(s))
            def _(s=s):
                pair_of(sent_a.at[0]).wait_send()
                pl.when(core == 1)(lambda: pair_of(x_send.at[s - slots[0]]).wait_send())

        for s in slots:
            sends = core >= 0 if s == 2 else jnp.where(core == 1, tm >= 2 - s, sends_x(s))
            for r in range(2):
                pl.when(jnp.logical_and(side_of(r), sends))(lambda: pair_of(sent_a.at[0]).wait_send())

        half = wv.at[:, :, :, pl.ds(0, local)]
        remote(half, half, w_send.at[0], w_recv.at[0], chan=other).wait_send()

    sent()
    other_half(w2, 1).wait_recv()
    wait_stats(1)
    make_norms(1, 4, params[2], params[3], params[4])

    def norm2(p, carry):
        for f in range(2):
            for r in range(2):
                norm_into(act2, 1 + r, 2 * p + f, hid[p, r, f * wide:(f + 1) * wide], 1)
        return carry

    def wait_halo(side):
        for later_block, some in ((False, halo.at[side, 1]), (True, halo.at[side])):
            @pl.when((tm >= 1) == later_block)
            def _(some=some):
                remote(some, some, sent_b.at[0], h_recv.at[side], chan=other).wait_recv()

    def norms2(p):
        for side in range(2):
            @pl.when((has_down, has_up)[side])
            def _(side=side):
                for f in range(2):
                    v = halo[side, p, f * wide:(f + 1) * wide].astype(F32)
                    norm_into(act2, (0, 3)[side], 2 * p + f, v, 1)

    def norms2_of(step, carry):
        norms2(1 - step)
        return carry

    lax.fori_loop(2 - pairs, 2, norm2, 0)
    pl.when(tm > 0)(lambda: inner(act2, 1, 0, 0, first2))
    for side in range(2):
        pl.when((has_down, has_up)[side])(lambda side=side: wait_halo(side))
    lax.fori_loop(0, pairs, norms2_of, 0)
    def last_swap(r):
        return remote(part.at[2, r], landed.at[2, r], sent_b.at[0], r_recv.at[2 + r], chan=other)

    def send_last():
        for r in range(2):
            last_swap(r).start()

    pl.when(tm > 0)(lambda: outer(act2, 1, 0, 0, first2, send_last, 2))

    @pl.when(tm == 0)
    def _():
        for r in range(2):
            split(2, r, taps(act2, 1, 0, first2, (r, r + 1, r + 2), (0, 1, 2)))
        send_last()


    spread = select[...]
    sent_stats(1)
    swap(1).wait_send()
    pl.when(tm >= 1)(lambda: swap(0).wait_send())
    for r in range(2):
        pl.when(side_of(r))(lambda r=r: edge_copy(r).wait_send())
        pl.when(jnp.logical_and(side_of(r), sends_x(1)))(lambda r=r: edge_next(r).wait_send())

    for r in range(2):
        last_swap(r).wait_recv()
        pairs_of = []
        for f in range(2):
            at_frame = slice(f * wide, (f + 1) * wide)
            v = lat[2, 1 + r, f].astype(F32) + (hid[2, r, at_frame] + landed[2, r, at_frame].astype(F32) + params[5])
            mix[f * 2 + r] = v.T
            for p in range(2):
                pair = [mix[f * 2 + r, pl.ds(2 * p + q, local // 4, stride=4), :].astype(BF16) for q in range(2)]
                pairs_of.append(jnp.concatenate(pair, axis=1))
        spreads = jnp.dot(jnp.concatenate(pairs_of, axis=0), spread, preferred_element_type=F32).astype(BF16)
        for i in range(4):
            out[i // 2, 2 * r + i % 2] = spreads[i * (local // 4):(i + 1) * (local // 4)]

    swap(2).wait_send()


def shards(tiles, blocks, latent, n1g, n1b, w1, c1b, n2g, n2b, w2, c2b):
    frames, rows, local, wide = latent.shape
    peers = tiles * blocks
    before = min(blocks - 1, 2)
    vmem = pl.BlockSpec(memory_space=pltpu.VMEM)
    hbm = pl.BlockSpec(memory_space=pl.ANY)
    dma = pltpu.SemaphoreType.DMA
    here = lambda v: pltpu.with_memory_space_constraint(v, pltpu.HBM)
    row = lambda v: here(v.reshape(1, local))
    flat = lambda v: here(v.reshape(27, C, local))
    return pl.pallas_call(
        functools.partial(kernel, tiles, blocks),
        out_shape=jax.ShapeDtypeStruct((frames, 2 * rows, local // 4, 2 * wide), BF16),
        in_specs=[hbm] * 9,
        out_specs=vmem,
        scratch_shapes=[
            pltpu.VMEM(latent.shape, BF16),
            pltpu.VMEM((2, 27, local, C), BF16),
            pltpu.VMEM((3, 4, 2, wide, local), BF16),
            pltpu.VMEM((3, 4, 6, wide, local), BF16),
            pltpu.VMEM((3, 4, 4, wide, local), BF16),
            pltpu.VMEM((2, 2, 2 * wide, C), F32),
            pltpu.VMEM((3, 2, 2 * wide, local), F32),
            pltpu.VMEM((2, 2 * wide, local), BF16),
            pltpu.VMEM((2, 2, 2 * wide, local), BF16),
            pltpu.VMEM((4, local, wide), F32),
            pltpu.VMEM((2 * wide, 2 * wide), BF16),
            pltpu.VMEM((6, 1, local), F32),
            pltpu.VMEM((2, 4, local), F32),
            pltpu.VMEM((2, peers, 4, local), F32),
            pltpu.VMEM((2, 8, local), F32),
            pltpu.VMEM((2, 8, local), F32),
            pltpu.VMEM((3, 2, 2 * wide, local), BF16),
            pltpu.VMEM((3, 2, 2 * wide, local), BF16),
            dma((1,)),
            dma((1,)),
            dma((1,)),
            dma((2,)),
            dma((before,)),
            dma((before, 2, 2)),
            dma((before + 1, 2)),
            dma((4,)),
            dma((2,)),
            dma((2,)),
            dma((1,)),
            dma((1,)),
        ],
        compiler_params=pltpu.CompilerParams(
            collective_id=0, has_side_effects=True, vmem_limit_bytes=48 * 1024 * 1024
        ),
        name="block",
    )(here(latent), row(n1g), row(n1b), flat(w1), row(c1b), row(n2g), row(n2b), flat(w2), row(c2b))


def solution(mesh):
    return jax.shard_map(
        functools.partial(shards, mesh.shape["tile"], mesh.shape["tm"]),
        mesh=mesh,
        in_specs=(
            P(("clip", "tm"), "tile", "chan", None),
            P("chan"),
            P("chan"),
            P(None, None, None, None, "chan"),
            P("chan"),
            P("chan"),
            P("chan"),
            P(None, None, None, None, "chan"),
            P("chan"),
        ),
        out_specs=P(("clip", "tm"), "tile", "chan", None),
        check_vma=False,
    )
```
